32 devices in a mesh: seq: 16 (over z, x, core), grp: 2 (over y).
Axes of the slice: x: 2, y: 2, z: 4, core: 2. Of those that a mesh axis runs over, the one named last changes fastest.
Arguments:
- values: bfloat16 [2, 4096, 512], P('grp', 'seq'), may hold values from -6 to 6
- gate: bfloat16 [2, 4096, 512], P('grp', 'seq'), may hold values from -6 to 6
- lengths: int32 [2], P('grp'), may hold values from 512 to 4096, as said below
- bands: int32 [16], replicated, may hold values from 1 to 1024
- w_in: float32 [33, 64], replicated, may hold values from -1 to 1
- b_in: float32 [64], replicated, may hold values from -3.140625 to 3.140625
- w_mid: float32 [64, 64], replicated, may hold values from -0.75 to 0.75
- w_out: float32 [64, 512], replicated, may hold values from -0.75 to 0.75
- decay: float32 [512], replicated, may hold values from 0.6 to 12
- skip: float32 [512], replicated, may hold values from 0.5 to 1.5
Outputs:
- filtered: bfloat16 [2, 4096, 512], P('grp', 'seq')
The draws below stay inside these ranges and needn't reach their ends.
Inputs may be any that keep to these rules, and one draw needn't show every extreme that they name: `lengths`: each sequence's length; some sequence fills all 4096 positions.
All inputs are finite; a program needn't handle non-finite values.
Results may differ from the reference program's by a relative error of at most 0.001.
Values sent between devices are 32-bit elements; how exact they have to be, the bound alone decides.
No kernel may reach another device: no remote copies, remote signals or barrier semaphores. Data moves between devices by JAX's collectives and lax.ppermute only.
A program may use at most 64 MiB of HBM per device.

```python
import math
import jax
import jax.numpy as jnp
from jax import lax

CH = 512
BANDS = 16
HID = 64
EMB = 33
LENGTH_ROW = 4096
ROWS = 2


def draw_lengths(key, part):
    key_len = jax.random.fold_in(key, 11)
    key_full = jax.random.fold_in(key, 12)
    drawn = jax.random.randint(key_len, (ROWS,), LENGTH_ROW // 8, LENGTH_ROW + 1)
    full_row = jax.random.randint(key_full, (), 0, ROWS)
    return jnp.where(jnp.arange(ROWS) == full_row, LENGTH_ROW, drawn).astype(jnp.int32)


def draw_decay(key, part):
    key_slow = jax.random.fold_in(key, 21)
    key_fast = jax.random.fold_in(key, 22)
    key_pick = jax.random.fold_in(key, 23)
    slow_rate = jnp.exp(jax.random.uniform(key_slow, (CH,), jnp.float32, math.log(0.6), math.log(2.2)))
    fast_rate = jnp.exp(jax.random.uniform(key_fast, (CH,), jnp.float32, math.log(4.0), math.log(12.0) - 0.0001))
    chosen = jax.random.uniform(key_pick, (CH,), jnp.float32) < 0.5
    return jnp.where(chosen, slow_rate, fast_rate).astype(jnp.float32)


def set_ends(values, key, least, largest):
    longest = values.shape.index(max(values.shape))
    spots = []
    for shift in (0, 1):
        where = [jax.random.randint(jax.random.fold_in(key, axis), (), 0, length) for axis, length in enumerate(values.shape)]
        where[longest] = (where[longest] + shift) % values.shape[longest]
        spots.append(tuple(where))
    return values.at[spots[0]].set(least).at[spots[1]].set(largest)


def levels(own_key, dims, pieces, smallest, high):
    level, own = 1.0, jax.random.fold_in(own_key, 6)
    for position, parts in pieces:
        heights = jnp.exp(jax.random.uniform(jax.random.fold_in(own, position), (parts,), jnp.float32, smallest / len(pieces), high / len(pieces)))
        level = level * jnp.repeat(heights, dims[position] // parts).reshape([-1 if axis == position else 1 for axis in range(len(dims))])
    return level


def centred(stream_key, extent, deviation, reach, split=(), kind=jnp.bfloat16):
    values = jax.random.normal(stream_key, extent, jnp.float32) * deviation
    if len(split) > 0:
        values = levels(stream_key, extent, split, -0.22, 0.18) * values
    return jnp.clip(values, min=-reach, max=reach).astype(kind)


def setup_inputs(seed: int = 0) -> dict:
    splits = jax.random.split(jax.random.key(seed), 11)
    return {
        "values": centred(splits[0], (ROWS, LENGTH_ROW, CH), 1.0, 6.0, ((0, 2), (1, 16))),
        "gate": centred(splits[1], (ROWS, LENGTH_ROW, CH), 1.0, 6.0, ((0, 2), (1, 16))),
        "lengths": draw_lengths(jax.random.fold_in(splits[10], 71), 0),
        "bands": set_ends(jax.random.randint(splits[3], (BANDS,), 1, LENGTH_ROW // 4 + 1), jax.random.fold_in(splits[3], 1), 1, (LENGTH_ROW // 4 + 1) - 1).astype(jnp.int32),
        "w_in": centred(splits[4], (EMB, HID), EMB ** -0.5, 1.0, (), jnp.float32),
        "b_in": jnp.clip(jax.random.uniform(splits[5], (HID,), jnp.float32, -3.140625, 3.140625), -3.140625, 3.140625),
        "w_mid": centred(splits[6], (HID, HID), HID ** -0.5, 0.75, (), jnp.float32),
        "w_out": centred(splits[7], (HID, CH), HID ** -0.5, 0.75, (), jnp.float32),
        "decay": draw_decay(jax.random.fold_in(splits[10], 71), 0),
        "skip": jnp.clip(jax.random.uniform(splits[9], (CH,), jnp.float32, 0.5, 1.5), 0.5, 1.5),
    }


TWO_PI = 2.0 * math.pi

def filter_rows(positions, row_len, bands, w_in, b_in, w_mid, w_out, decay):
    times = positions.astype(jnp.float32) / row_len
    phase = (positions[None, :] * bands[:, None] % row_len).astype(jnp.float32) * (TWO_PI / row_len)
    embed = jnp.concatenate([times[None, :], jnp.sin(phase), jnp.cos(phase)], axis=0)
    contract = (((0,), (0,)), ((), ()))
    first = jnp.sin(lax.dot_general(w_in, embed, contract, precision=lax.Precision.HIGHEST) + b_in[:, None])
    second = jnp.sin(lax.dot_general(w_mid, first, contract, precision=lax.Precision.HIGHEST))
    raw = lax.dot_general(second, w_out, contract, precision=lax.Precision.HIGHEST)
    return raw * jnp.exp(-decay[None, :] * times[:, None])

def reference(values, gate, lengths, bands, w_in, b_in, w_mid, w_out, decay, skip):
    positions = jnp.arange(LENGTH_ROW, dtype=jnp.int32)
    shaped = filter_rows(positions, LENGTH_ROW, bands, w_in, b_in, w_mid, w_out, decay)
    energy = lax.optimization_barrier(jnp.sum(shaped * shaped, axis=0))
    kernel = shaped * lax.rsqrt(energy + 1e-06)
    kernel_spec = jnp.fft.rfft(kernel, n=2 * LENGTH_ROW, axis=0)

    def one_row(operands):
        row_values, row_gate, row_length = operands
        live = (positions < row_length).astype(jnp.float32)[:, None]
        masked = row_values.astype(jnp.float32) * live
        conv = jnp.fft.irfft(jnp.fft.rfft(masked, n=2 * LENGTH_ROW, axis=0) * kernel_spec, n=2 * LENGTH_ROW, axis=0)[:LENGTH_ROW]
        result = row_gate.astype(jnp.float32) * (conv + skip[None, :] * masked) * live
        return result.astype(jnp.bfloat16)
    return lax.map(one_row, (values, gate, lengths))
```

```python
import functools
import math

import jax
import jax.numpy as jnp
import ml_dtypes
import numpy as np
from jax import lax
from jax.experimental import pallas as pl
from jax.experimental.pallas import tpu as pltpu
from jax.sharding import PartitionSpec as P

F32 = jnp.float32
BF16 = jnp.bfloat16
VMEM_LIMIT = 48 * 1024 * 1024


def split_np(table):
    high = table.astype(np.float32).astype(ml_dtypes.bfloat16)
    low = (table - high.astype(np.float64)).astype(np.float32).astype(ml_dtypes.bfloat16)
    return high, low


def dft_tables(q):
    f = np.arange(q)[None, :]
    n = np.arange(q)[:, None]
    turn = 2.0 * math.pi / (4 * q)
    ahead = ((2 * f + 1) * n % (4 * q)) * turn
    forward = np.concatenate([np.cos(ahead), -np.sin(ahead)], axis=1)
    back = ((2 * f.T + 1) * (n.T + q) % (4 * q)) * turn
    inverse = np.concatenate([np.cos(back), -np.sin(back)], axis=0) / q
    return split_np(forward) + split_np(inverse)


def split(x):
    high = x.astype(BF16)
    return high, (x - high.astype(F32)).astype(BF16)


def dot(a, b, precision=None):
    return lax.dot_general(
        a, b, (((1,), (0,)), ((), ())), precision=precision, preferred_element_type=F32
    )


def dot3(a, b_high, b_low):
    a_high, a_low = split(a)
    return dot(a_high, b_high) + dot(a_low, b_high) + dot(a_high, b_low)


PI_A = 3.140625
PI_B = 9.67502593994140625e-4
PI_C = math.pi - PI_A - PI_B


def odd_fit(func, reach, terms):
    nodes = np.cos(np.pi * (np.arange(400) + 0.5) / 400) * reach
    nodes = nodes[nodes > 0]
    basis = np.stack([nodes ** (2 * i + 1) for i in range(terms)], axis=1)
    weight = 1.0 / nodes[:, None] ** 0.5
    return np.linalg.lstsq(basis * weight, func(nodes) * weight[:, 0], rcond=None)[0]


def even_fit(func, reach, terms):
    nodes = np.cos(np.pi * (np.arange(400) + 0.5) / 400) * reach
    basis = np.stack([nodes ** (2 * i) for i in range(terms)], axis=1)
    return np.linalg.lstsq(basis, func(nodes), rcond=None)[0]


SIN_HALF = [float(c) for c in odd_fit(np.sin, math.pi / 2, 6)]
SIN_QUARTER = [float(c) for c in odd_fit(np.sin, math.pi / 4, 4)]
COS_QUARTER = [float(c) for c in even_fit(np.cos, math.pi / 4, 5)]


def horner(square, coefficients):
    total = jnp.full_like(square, coefficients[-1])
    for c in coefficients[-2::-1]:
        total = total * square + c
    return total


def sine(x):
    turns = lax.round(x * (1.0 / math.pi), lax.RoundingMethod.TO_NEAREST_EVEN)
    r = ((x - turns * PI_A) - turns * PI_B) - turns * PI_C
    value = r * horner(r * r, SIN_HALF)
    odd = (turns.astype(jnp.int32) & 1) == 1
    return jnp.where(odd, -value, value)


def sine_cosine(step, row_len):
    quarter = row_len // 4
    corner = (step + quarter // 2) // quarter
    r = (step - corner * quarter).astype(F32) * (2.0 * math.pi / row_len)
    square = r * r
    s = r * horner(square, SIN_QUARTER)
    c = horner(square, COS_QUARTER)
    swap = (corner & 1) == 1
    sin_v = jnp.where(swap, c, s)
    cos_v = jnp.where(swap, s, c)
    sin_v = jnp.where((corner & 2) == 2, -sin_v, sin_v)
    cos_v = jnp.where(((corner + 1) & 2) == 2, -cos_v, cos_v)
    return sin_v, cos_v


def send_kernel(start_ref, len_ref, x_ref, o_ref):
    rows, channels = x_ref.shape
    room = len_ref[0] - start_ref[0]
    position = lax.broadcasted_iota(jnp.int32, (rows, channels), 0)
    masked = jnp.where(position < room, x_ref[...].astype(F32), 0.0)
    o_ref[...] = masked.T


def filter_kernel(
    row_len, q, own, start_ref, bands_ref, w_in_ref, b_in_ref, w_mid_ref, w_out_ref, decay_ref,
    fh_ref, fl_ref, g_ref, wide_ref, turned_ref, embed_ref, shaped_ref, spec_ref,
):
    hid = w_mid_ref.shape[0]
    bands = bands_ref.shape[0]
    emb = w_in_ref.shape[0]
    channels = w_out_ref.shape[1]
    blocks = row_len // q
    high = lax.Precision.HIGHEST
    depth = embed_ref.shape[0]

    wide_ref[...] = jnp.zeros_like(wide_ref)
    wide_ref[0 : 2 * bands, 0:hid] = w_in_ref[1:emb, :]
    wide_ref[2 * bands : 2 * bands + 1, 0:hid] = w_in_ref[0:1, :]
    wide_ref[2 * bands + 1 : 2 * bands + 2, 0:hid] = b_in_ref[...]
    w_first = wide_ref[...].T[0:hid, 0:depth]
    wide_ref[...] = jnp.zeros_like(wide_ref)
    wide_ref[0:hid, 0:hid] = w_mid_ref[...]
    w_second = wide_ref[...].T[0:hid, 0:hid]
    turned_ref[:, 0:hid] = w_out_ref[...].T
    turned_ref[:, hid : hid + 8] = jnp.broadcast_to(decay_ref[...], (8, channels)).T
    mine = pl.ds(pl.multiple_of(start_ref[0], own), own)
    w_last = turned_ref[mine, 0:hid]
    rate = turned_ref[mine, hid : hid + 1]

    row = lax.broadcasted_iota(jnp.int32, (bands, 128), 0)
    column = jnp.zeros((bands, 128), jnp.int32)
    for k in range(bands):
        column = jnp.where(row == k, bands_ref[k], column)
    column = column[:, 0:1]

    chunk = min(1024, row_len)
    energy = jnp.zeros((own, 1), F32)
    for begin in range(0, row_len, chunk):
        at = slice(begin, begin + chunk)
        position = lax.broadcasted_iota(jnp.int32, (1, chunk), 1) + begin
        time = position.astype(F32) * (1.0 / row_len)
        step = lax.rem(
            (lax.broadcasted_iota(jnp.int32, (bands, chunk), 1) + begin) * column,
            jnp.int32(row_len),
        ) if row_len & (row_len - 1) else (
            (lax.broadcasted_iota(jnp.int32, (bands, chunk), 1) + begin) * column & (row_len - 1)
        )
        sin_v, cos_v = sine_cosine(step, row_len)
        embed_ref[0:bands, at] = sin_v
        embed_ref[bands : 2 * bands, at] = cos_v
        tail = lax.broadcasted_iota(jnp.int32, (depth - 2 * bands, chunk), 0)
        embed_ref[2 * bands : depth, at] = jnp.where(
            tail == 0, time, jnp.where(tail == 1, 1.0, 0.0)
        )
        first = sine(dot(w_first, embed_ref[:, at], high))
        second = sine(dot(w_second, first, high))
        shaped = dot(w_last, second, high) * jnp.exp(-rate * time)
        shaped_ref[:, at] = shaped
        energy = energy + jnp.sum(shaped * shaped, axis=1, keepdims=True)
    scale = lax.rsqrt(energy + 1e-06)
    rows = jnp.concatenate(
        [shaped_ref[:, d * q : (d + 1) * q] * scale for d in range(blocks)], axis=0
    )
    spec_ref[...] = dot3(rows, fh_ref[...], fl_ref[...])
    sign = (1 - 2 * (lax.broadcasted_iota(jnp.int32, (own, q), 1) & 1)).astype(F32)
    for d in range(blocks):
        here = slice(d * own, (d + 1) * own)
        re = sign * spec_ref[here, q : 2 * q]
        im = -sign * spec_ref[here, 0:q]
        if d:
            before = slice((d - 1) * own, d * own)
            re = re + spec_ref[before, 0:q]
            im = im + spec_ref[before, q : 2 * q]
        g_ref[here, 0:q] = re
        g_ref[here, q : 2 * q] = im


def conv_kernel(q, own, x_ref, g_ref, fh_ref, fl_ref, ih_ref, il_ref, o_ref, spec_ref, prod_ref):
    blocks = x_ref.shape[0] // own
    x = x_ref[...].astype(BF16)
    spec_ref[...] = dot(x, fh_ref[...]) + dot(x, fl_ref[...])
    tile_r, tile_c = 8, 128
    for r in range(own // tile_r):
        for c in range(q // tile_c):
            re_at = slice(c * tile_c, (c + 1) * tile_c)
            im_at = slice(q + c * tile_c, q + (c + 1) * tile_c)
            at = [slice(b * own + r * tile_r, b * own + (r + 1) * tile_r) for b in range(blocks)]
            for b in range(blocks):
                rr = ii = ri = ir = None
                for a in range(b + 1):
                    g_re, g_im = g_ref[at[b - a], re_at], g_ref[at[b - a], im_at]
                    x_re, x_im = spec_ref[at[a], re_at], spec_ref[at[a], im_at]
                    terms = (g_re * x_re, g_im * x_im, g_re * x_im, g_im * x_re)
                    if rr is None:
                        rr, ii, ri, ir = terms
                    else:
                        rr, ii, ri, ir = rr + terms[0], ii + terms[1], ri + terms[2], ir + terms[3]
                prod_ref[at[b], re_at] = rr - ii
                prod_ref[at[b], im_at] = ri + ir
    o_ref[...] = dot3(prod_ref[...], ih_ref[...], il_ref[...])


def finish_kernel(start_ref, len_ref, conv_ref, x_ref, gate_ref, skip_ref, o_ref):
    rows, channels = x_ref.shape
    room = len_ref[0] - start_ref[0]
    live = lax.broadcasted_iota(jnp.int32, (rows, channels), 0) < room
    masked = jnp.where(live, x_ref[...].astype(F32), 0.0)
    result = gate_ref[...].astype(F32) * (conv_ref[...].T + skip_ref[...] * masked)
    o_ref[...] = jnp.where(live, result, 0.0).astype(BF16)


def call(body, out, smem, vmem, scratch=(), flops=0, moved=0, **kwargs):
    return pl.pallas_call(
        body,
        out_shape=out,
        in_specs=[pl.BlockSpec(memory_space=pltpu.SMEM)] * smem
        + [pl.BlockSpec(memory_space=pltpu.VMEM)] * vmem,
        out_specs=pl.BlockSpec(memory_space=pltpu.VMEM),
        scratch_shapes=list(scratch),
        compiler_params=pltpu.CompilerParams(vmem_limit_bytes=VMEM_LIMIT),
        cost_estimate=pl.CostEstimate(flops=flops, bytes_accessed=moved, transcendentals=0),
        **kwargs,
    )


def on_device(values, gate, lengths, bands, w_in, b_in, w_mid, w_out, decay, skip):
    seq_count = lax.axis_size("seq")
    seq_pos = lax.axis_index("seq")
    q, channels = values.shape[1:]
    own = channels // seq_count
    row_len = q * seq_count
    hid = w_mid.shape[0]
    start = (seq_pos * q).astype(jnp.int32).reshape(1)
    first_channel = (seq_pos * own).astype(jnp.int32).reshape(1)
    fh, fl, ih, il = (jnp.asarray(t) for t in dft_tables(q))

    outgoing = call(
        send_kernel, jax.ShapeDtypeStruct((channels, q), F32), 2, 1, moved=3 * q * channels * 2
    )(start, lengths, values[0])
    incoming = lax.all_to_all(
        outgoing.reshape(seq_count, own, q), "seq", split_axis=0, concat_axis=0, tiled=True
    ).reshape(channels, q)

    depth = -(-(w_in.shape[0] + 1) // 8) * 8
    spectrum = call(
        functools.partial(filter_kernel, row_len, q, own),
        jax.ShapeDtypeStruct((channels, 2 * q), F32),
        2,
        7,
        scratch=[
            pltpu.VMEM((128, 128), F32),
            pltpu.VMEM((channels, 128), F32),
            pltpu.VMEM((depth, row_len), F32),
            pltpu.VMEM((own, row_len), F32),
            pltpu.VMEM((channels, 2 * q), F32),
        ],
        flops=6 * 2 * row_len * hid * 256 * 8,
        moved=4 * channels * 2 * q,
    )(first_channel, bands, w_in, b_in.reshape(1, hid), w_mid, w_out, decay.reshape(1, channels), fh, fl)

    convolved = call(
        functools.partial(conv_kernel, q, own),
        jax.ShapeDtypeStruct((channels, q), F32),
        0,
        6,
        scratch=[pltpu.VMEM((channels, 2 * q), F32), pltpu.VMEM((channels, 2 * q), F32)],
        flops=5 * 4 * channels * q * q,
        moved=16 * channels * q,
    )(incoming, spectrum, fh, fl, ih, il)
    returned = lax.all_to_all(
        convolved.reshape(seq_count, own, q), "seq", split_axis=0, concat_axis=0, tiled=True
    ).reshape(channels, q)
    return call(
        finish_kernel, jax.ShapeDtypeStruct((q, channels), BF16), 2, 4, moved=10 * q * channels
    )(start, lengths, returned, values[0], gate[0], skip.reshape(1, channels))[None]


def solution(mesh):
    split_spec = P("grp", "seq", None)
    return jax.shard_map(
        on_device,
        mesh=mesh,
        in_specs=(split_spec, split_spec, P("grp")) + (P(),) * 7,
        out_specs=split_spec,
        check_vma=False,
    )
```

```python
import functools
import math

import jax
import jax.numpy as jnp
import ml_dtypes
import numpy as np
from jax import lax
from jax.experimental import pallas as pl
from jax.experimental.pallas import tpu as pltpu
from jax.sharding import PartitionSpec as P

F32 = jnp.float32
BF16 = jnp.bfloat16
VMEM_LIMIT = 48 * 1024 * 1024


def split_np(table):
    high = table.astype(np.float32).astype(ml_dtypes.bfloat16)
    low = (table - high.astype(np.float64)).astype(np.float32).astype(ml_dtypes.bfloat16)
    return high, low


def dft_tables(q):
    f = np.arange(q)[None, :]
    n = np.arange(q)[:, None]
    turn = 2.0 * math.pi / (4 * q)
    ahead = ((2 * f + 1) * n % (4 * q)) * turn
    forward = np.concatenate([np.cos(ahead), -np.sin(ahead)], axis=1)
    back = ((2 * f.T + 1) * (n.T + q) % (4 * q)) * turn
    inverse = np.concatenate([np.cos(back), -np.sin(back)], axis=0) / q
    return split_np(forward) + split_np(inverse)


def split(x):
    high = x.astype(BF16)
    return high, (x - high.astype(F32)).astype(BF16)


def dot(a, b, precision=None):
    return lax.dot_general(
        a, b, (((1,), (0,)), ((), ())), precision=precision, preferred_element_type=F32
    )


def dot3(a, b_high, b_low):
    a_high, a_low = split(a)
    return dot(a_high, b_high) + dot(a_low, b_high) + dot(a_high, b_low)


PI_A = 3.140625
PI_B = 9.67502593994140625e-4
PI_C = math.pi - PI_A - PI_B


def odd_fit(func, reach, terms):
    nodes = np.cos(np.pi * (np.arange(400) + 0.5) / 400) * reach
    nodes = nodes[nodes > 0]
    basis = np.stack([nodes ** (2 * i + 1) for i in range(terms)], axis=1)
    weight = 1.0 / nodes[:, None] ** 0.5
    return np.linalg.lstsq(basis * weight, func(nodes) * weight[:, 0], rcond=None)[0]


def even_fit(func, reach, terms):
    nodes = np.cos(np.pi * (np.arange(400) + 0.5) / 400) * reach
    basis = np.stack([nodes ** (2 * i) for i in range(terms)], axis=1)
    return np.linalg.lstsq(basis, func(nodes), rcond=None)[0]


SIN_HALF = [float(c) for c in odd_fit(np.sin, math.pi / 2, 6)]
SIN_QUARTER = [float(c) for c in odd_fit(np.sin, math.pi / 4, 4)]
COS_QUARTER = [float(c) for c in even_fit(np.cos, math.pi / 4, 5)]


def horner(square, coefficients):
    total = jnp.full_like(square, coefficients[-1])
    for c in coefficients[-2::-1]:
        total = total * square + c
    return total


def sine(x):
    turns = lax.round(x * (1.0 / math.pi), lax.RoundingMethod.TO_NEAREST_EVEN)
    r = ((x - turns * PI_A) - turns * PI_B) - turns * PI_C
    value = r * horner(r * r, SIN_HALF)
    odd = (turns.astype(jnp.int32) & 1) == 1
    return jnp.where(odd, -value, value)


def sine_cosine(step, row_len):
    quarter = row_len // 4
    corner = (step + quarter // 2) // quarter
    r = (step - corner * quarter).astype(F32) * (2.0 * math.pi / row_len)
    square = r * r
    s = r * horner(square, SIN_QUARTER)
    c = horner(square, COS_QUARTER)
    swap = (corner & 1) == 1
    sin_v = jnp.where(swap, c, s)
    cos_v = jnp.where(swap, s, c)
    sin_v = jnp.where((corner & 2) == 2, -sin_v, sin_v)
    cos_v = jnp.where(((corner + 1) & 2) == 2, -cos_v, cos_v)
    return sin_v, cos_v


def send_kernel(start_ref, len_ref, x_ref, o_ref):
    rows, channels = x_ref.shape
    live = lax.broadcasted_iota(jnp.int32, (1, rows), 1) < len_ref[0] - start_ref[0]
    o_ref[...] = jnp.where(live, x_ref[...].T.astype(F32), 0.0)


def filter_kernel(
    row_len, q, own, start_ref, bands_ref, w_in_ref, b_in_ref, w_mid_ref, w_out_ref, decay_ref,
    skip_ref, fh_ref, fl_ref, g_ref, wide_ref, turned_ref, embed_ref, shaped_ref, spec_ref,
):
    hid = w_mid_ref.shape[0]
    bands = bands_ref.shape[0]
    emb = w_in_ref.shape[0]
    channels = w_out_ref.shape[1]
    blocks = row_len // q
    high = lax.Precision.HIGHEST
    depth = embed_ref.shape[0]

    wide_ref[...] = jnp.zeros_like(wide_ref)
    wide_ref[0 : 2 * bands, 0:hid] = w_in_ref[1:emb, :]
    wide_ref[2 * bands : 2 * bands + 1, 0:hid] = w_in_ref[0:1, :]
    wide_ref[2 * bands + 1 : 2 * bands + 2, 0:hid] = b_in_ref[...]
    w_first = wide_ref[...].T[0:hid, 0:depth]
    wide_ref[...] = jnp.zeros_like(wide_ref)
    wide_ref[0:hid, 0:hid] = w_mid_ref[...]
    w_second = wide_ref[...].T[0:hid, 0:hid]
    turned_ref[:, 0:hid] = w_out_ref[...].T
    turned_ref[:, hid : hid + 8] = jnp.broadcast_to(decay_ref[...], (8, channels)).T
    turned_ref[:, hid + 8 : hid + 16] = jnp.broadcast_to(skip_ref[...], (8, channels)).T
    mine = pl.ds(pl.multiple_of(start_ref[0], own), own)
    w_last = turned_ref[mine, 0:hid]
    rate = turned_ref[mine, hid : hid + 1]
    direct = turned_ref[mine, hid + 8 : hid + 9]

    row = lax.broadcasted_iota(jnp.int32, (bands, 128), 0)
    column = jnp.zeros((bands, 128), jnp.int32)
    for k in range(bands):
        column = jnp.where(row == k, bands_ref[k], column)
    column = column[:, 0:1]

    chunk = min(1024, row_len)
    energy = jnp.zeros((own, 1), F32)
    for begin in range(0, row_len, chunk):
        at = slice(begin, begin + chunk)
        position = lax.broadcasted_iota(jnp.int32, (1, chunk), 1) + begin
        time = position.astype(F32) * (1.0 / row_len)
        step = lax.rem(
            (lax.broadcasted_iota(jnp.int32, (bands, chunk), 1) + begin) * column,
            jnp.int32(row_len),
        ) if row_len & (row_len - 1) else (
            (lax.broadcasted_iota(jnp.int32, (bands, chunk), 1) + begin) * column & (row_len - 1)
        )
        sin_v, cos_v = sine_cosine(step, row_len)
        embed_ref[0:bands, at] = sin_v
        embed_ref[bands : 2 * bands, at] = cos_v
        tail = lax.broadcasted_iota(jnp.int32, (depth - 2 * bands, chunk), 0)
        embed_ref[2 * bands : depth, at] = jnp.where(
            tail == 0, time, jnp.where(tail == 1, 1.0, 0.0)
        )
        first = sine(dot(w_first, embed_ref[:, at], high))
        second = sine(dot(w_second, first, high))
        shaped = dot(w_last, second, high) * jnp.exp(-rate * time)
        shaped_ref[:, at] = shaped
        energy = energy + jnp.sum(shaped * shaped, axis=1, keepdims=True)
    scale = lax.rsqrt(energy + 1e-06)
    first_lag = lax.broadcasted_iota(jnp.int32, (own, q), 1) == 0
    rows = [shaped_ref[:, d * q : (d + 1) * q] * scale for d in range(blocks)]
    rows[0] = rows[0] + jnp.where(first_lag, direct, 0.0)
    rows = jnp.concatenate(rows, axis=0)
    spec_ref[...] = dot3(rows, fh_ref[...], fl_ref[...])
    sign = (1 - 2 * (lax.broadcasted_iota(jnp.int32, (own, q), 1) & 1)).astype(F32)
    for d in range(blocks):
        here = slice(d * own, (d + 1) * own)
        re = sign * spec_ref[here, q : 2 * q]
        im = -sign * spec_ref[here, 0:q]
        if d:
            before = slice((d - 1) * own, d * own)
            re = re + spec_ref[before, 0:q]
            im = im + spec_ref[before, q : 2 * q]
        g_ref[here, 0:q] = re
        g_ref[here, q : 2 * q] = im - re
        g_ref[here, 2 * q : 3 * q] = re + im


def conv_kernel(q, own, x_ref, g_ref, fh_ref, fl_ref, ih_ref, il_ref, o_ref, spec_ref, prod_ref):
    blocks = x_ref.shape[0] // own
    groups, lanes, pair = own // 8, 128, 2
    for h in range(groups):
        rows = [x_ref[b * own + h * 8 : b * own + h * 8 + 8, :] for b in range(blocks)]
        x = jnp.concatenate(rows, axis=0).astype(BF16)
        re = dot(x, fh_ref[:, 0:q]) + dot(x, fl_ref[:, 0:q])
        im = dot(x, fh_ref[:, q : 2 * q]) + dot(x, fl_ref[:, q : 2 * q])
        at = slice(h * blocks * 8, (h + 1) * blocks * 8)
        spec_ref[at, 0:q] = re
        spec_ref[at, q : 2 * q] = im
        spec_ref[at, 2 * q : 3 * q] = re + im
    for h in range(groups):
        here = [slice((h * blocks + b) * 8, (h * blocks + b + 1) * 8) for b in range(blocks)]
        there = [slice(b * own + h * 8, b * own + h * 8 + 8) for b in range(blocks)]
        for c in range(0, q, lanes):
            planes = [slice(p * q + c, p * q + c + lanes) for p in range(3)]
            for begin in range(0, blocks, pair):
                total = {}
                for a in range(begin + pair):
                    x_re, x_im, x_sum = (spec_ref[here[a], p] for p in planes)
                    for b in range(max(begin, a), begin + pair):
                        g_re, g_diff, g_sum = (g_ref[there[b - a], p] for p in planes)
                        terms = (g_re * x_sum, g_diff * x_re, g_sum * x_im)
                        total[b] = [t + u for t, u in zip(total[b], terms)] if b in total else terms
                for b in range(begin, begin + pair):
                    both, up, down = total[b]
                    prod_ref[here[b], planes[0]] = both - down
                    prod_ref[here[b], planes[1]] = both + up
        y = dot3(prod_ref[h * blocks * 8 : (h + 1) * blocks * 8, :], ih_ref[...], il_ref[...])
        for b in range(blocks):
            o_ref[there[b], :] = y[b * 8 : (b + 1) * 8, :]


def finish_kernel(start_ref, len_ref, conv_ref, gate_ref, o_ref):
    rows, channels = gate_ref.shape
    room = len_ref[0] - start_ref[0]
    live = lax.broadcasted_iota(jnp.int32, (rows, channels), 0) < room
    result = gate_ref[...].astype(F32) * conv_ref[...].T
    o_ref[...] = jnp.where(live, result, 0.0).astype(BF16)


def call(body, out, smem, vmem, scratch=(), flops=0, moved=0, **kwargs):
    return pl.pallas_call(
        body,
        out_shape=out,
        in_specs=[pl.BlockSpec(memory_space=pltpu.SMEM)] * smem
        + [pl.BlockSpec(memory_space=pltpu.VMEM)] * vmem,
        out_specs=pl.BlockSpec(memory_space=pltpu.VMEM),
        scratch_shapes=list(scratch),
        compiler_params=pltpu.CompilerParams(vmem_limit_bytes=VMEM_LIMIT),
        cost_estimate=pl.CostEstimate(flops=flops, bytes_accessed=moved, transcendentals=0),
        **kwargs,
    )


def on_device(values, gate, lengths, bands, w_in, b_in, w_mid, w_out, decay, skip):
    seq_count = lax.axis_size("seq")
    seq_pos = lax.axis_index("seq")
    q, channels = values.shape[1:]
    own = channels // seq_count
    row_len = q * seq_count
    hid = w_mid.shape[0]
    start = (seq_pos * q).astype(jnp.int32).reshape(1)
    first_channel = (seq_pos * own).astype(jnp.int32).reshape(1)
    fh, fl, ih, il = (jnp.asarray(t) for t in dft_tables(q))

    outgoing = call(
        send_kernel, pltpu.VMEM((channels, q), F32), 2, 1, moved=3 * q * channels * 2
    )(start, lengths, values[0])
    incoming = lax.all_to_all(
        outgoing.reshape(seq_count, own, q), "seq", split_axis=0, concat_axis=0, tiled=True
    ).reshape(channels, q)

    depth = -(-(w_in.shape[0] + 1) // 8) * 8
    spectrum = call(
        functools.partial(filter_kernel, row_len, q, own),
        jax.ShapeDtypeStruct((channels, 3 * q), F32),
        2,
        8,
        scratch=[
            pltpu.VMEM((128, 128), F32),
            pltpu.VMEM((channels, 128), F32),
            pltpu.VMEM((depth, row_len), F32),
            pltpu.VMEM((own, row_len), F32),
            pltpu.VMEM((channels, 2 * q), F32),
        ],
        flops=6 * 2 * row_len * hid * 256 * 8,
        moved=4 * channels * 2 * q,
    )(first_channel, bands, w_in, b_in.reshape(1, hid), w_mid, w_out, decay.reshape(1, channels),
      skip.reshape(1, channels), fh, fl)

    convolved = call(
        functools.partial(conv_kernel, q, own),
        jax.ShapeDtypeStruct((channels, q), F32),
        0,
        6,
        scratch=[pltpu.VMEM((channels, 3 * q), F32), pltpu.VMEM((channels, 2 * q), F32)],
        flops=5 * 4 * channels * q * q,
        moved=16 * channels * q,
    )(incoming, spectrum, fh, fl, ih, il)
    returned = lax.all_to_all(
        convolved.reshape(seq_count, own, q), "seq", split_axis=0, concat_axis=0, tiled=True
    ).reshape(channels, q)
    return call(
        finish_kernel, jax.ShapeDtypeStruct((q, channels), BF16), 2, 2, moved=8 * q * channels
    )(start, lengths, returned, gate[0])[None]


def solution(mesh):
    split_spec = P("grp", "seq", None)
    return jax.shard_map(
        on_device,
        mesh=mesh,
        in_specs=(split_spec, split_spec, P("grp")) + (P(),) * 7,
        out_specs=split_spec,
        check_vma=False,
    )
```

```python
import functools
import math

import jax
import jax.numpy as jnp
import ml_dtypes
import numpy as np
from jax import lax
from jax.experimental import pallas as pl
from jax.experimental.pallas import tpu as pltpu
from jax.sharding import PartitionSpec as P

F32 = jnp.float32
BF16 = jnp.bfloat16
VMEM_LIMIT = 48 * 1024 * 1024


def split_np(table):
    high = table.astype(np.float32).astype(ml_dtypes.bfloat16)
    low = (table - high.astype(np.float64)).astype(np.float32).astype(ml_dtypes.bfloat16)
    return high, low


def dft_tables(q):
    f = np.arange(q)[None, :]
    n = np.arange(q)[:, None]
    turn = 2.0 * math.pi / (4 * q)
    ahead = ((2 * f + 1) * n % (4 * q)) * turn
    forward = np.concatenate([np.cos(ahead), -np.sin(ahead)], axis=1)
    back = ((2 * f.T + 1) * (n.T + q) % (4 * q)) * turn
    inverse = np.concatenate([np.cos(back), -np.sin(back)], axis=0) / q
    return split_np(forward) + split_np(inverse)


def split(x):
    high = x.astype(BF16)
    return high, (x - high.astype(F32)).astype(BF16)


def dot(a, b, precision=None):
    return lax.dot_general(
        a, b, (((1,), (0,)), ((), ())), precision=precision, preferred_element_type=F32
    )


def dot3(a, b_high, b_low):
    a_high, a_low = split(a)
    return dot(a_high, b_high) + dot(a_low, b_high) + dot(a_high, b_low)


PI_A = 3.140625
PI_B = 9.67502593994140625e-4
PI_C = math.pi - PI_A - PI_B


def odd_fit(func, reach, terms):
    nodes = np.cos(np.pi * (np.arange(400) + 0.5) / 400) * reach
    nodes = nodes[nodes > 0]
    basis = np.stack([nodes ** (2 * i + 1) for i in range(terms)], axis=1)
    weight = 1.0 / nodes[:, None] ** 0.5
    return np.linalg.lstsq(basis * weight, func(nodes) * weight[:, 0], rcond=None)[0]


def even_fit(func, reach, terms):
    nodes = np.cos(np.pi * (np.arange(400) + 0.5) / 400) * reach
    basis = np.stack([nodes ** (2 * i) for i in range(terms)], axis=1)
    return np.linalg.lstsq(basis, func(nodes), rcond=None)[0]


SIN_HALF = [float(c) for c in odd_fit(np.sin, math.pi / 2, 6)]
SIN_QUARTER = [float(c) for c in odd_fit(np.sin, math.pi / 4, 4)]
COS_QUARTER = [float(c) for c in even_fit(np.cos, math.pi / 4, 5)]


def horner(square, coefficients):
    total = jnp.full_like(square, coefficients[-1])
    for c in coefficients[-2::-1]:
        total = total * square + c
    return total


def sine(x):
    turns = lax.round(x * (1.0 / math.pi), lax.RoundingMethod.TO_NEAREST_EVEN)
    r = ((x - turns * PI_A) - turns * PI_B) - turns * PI_C
    value = r * horner(r * r, SIN_HALF)
    odd = (turns.astype(jnp.int32) & 1) == 1
    return jnp.where(odd, -value, value)


def sine_cosine(step, row_len):
    quarter = row_len // 4
    corner = (step + quarter // 2) // quarter
    r = (step - corner * quarter).astype(F32) * (2.0 * math.pi / row_len)
    square = r * r
    s = r * horner(square, SIN_QUARTER)
    c = horner(square, COS_QUARTER)
    swap = (corner & 1) == 1
    sin_v = jnp.where(swap, c, s)
    cos_v = jnp.where(swap, s, c)
    sin_v = jnp.where((corner & 2) == 2, -sin_v, sin_v)
    cos_v = jnp.where(((corner + 1) & 2) == 2, -cos_v, cos_v)
    return sin_v, cos_v


def turned_live(x, count, room):
    q, channels = x.shape
    row = lax.broadcasted_iota(jnp.int32, (q, q), 0)
    column = lax.broadcasted_iota(jnp.int32, (q, q), 1)
    keep = jnp.where((row == column) & (row < room), 1.0, 0.0).astype(BF16)
    return lax.dot_general(
        x.reshape(q, count, channels // count),
        keep,
        (((0,), (0,)), ((), ())),
        preferred_element_type=F32,
    )


def filter_kernel(
    row_len, q, own, start_ref, bands_ref, w_in_ref, b_in_ref, w_mid_ref, w_out_ref, decay_ref,
    skip_ref, fh_ref, fl_ref, g_ref, wide_ref, turned_ref, embed_ref, shaped_ref, spec_ref,
):
    hid = w_mid_ref.shape[0]
    bands = bands_ref.shape[0]
    emb = w_in_ref.shape[0]
    channels = w_out_ref.shape[1]
    blocks = row_len // q
    high = lax.Precision.HIGHEST
    depth = embed_ref.shape[0]

    wide_ref[...] = jnp.zeros_like(wide_ref)
    wide_ref[0 : 2 * bands, 0:hid] = w_in_ref[1:emb, :]
    wide_ref[2 * bands : 2 * bands + 1, 0:hid] = w_in_ref[0:1, :]
    wide_ref[2 * bands + 1 : 2 * bands + 2, 0:hid] = b_in_ref[...]
    w_first = wide_ref[...].T[0:hid, 0:depth]
    wide_ref[...] = jnp.zeros_like(wide_ref)
    wide_ref[0:hid, 0:hid] = w_mid_ref[...]
    w_second = wide_ref[...].T[0:hid, 0:hid]
    turned_ref[:, 0:hid] = w_out_ref[...].T
    turned_ref[:, hid : hid + 8] = jnp.broadcast_to(decay_ref[...], (8, channels)).T
    turned_ref[:, hid + 8 : hid + 16] = jnp.broadcast_to(skip_ref[...], (8, channels)).T
    mine = pl.ds(pl.multiple_of(start_ref[0], own), own)
    w_last = turned_ref[mine, 0:hid]
    rate = turned_ref[mine, hid : hid + 1]
    direct = turned_ref[mine, hid + 8 : hid + 9]

    row = lax.broadcasted_iota(jnp.int32, (bands, 128), 0)
    column = jnp.zeros((bands, 128), jnp.int32)
    for k in range(bands):
        column = jnp.where(row == k, bands_ref[k], column)
    column = column[:, 0:1]

    chunk = min(1024, row_len)
    energy = jnp.zeros((own, 1), F32)
    for begin in range(0, row_len, chunk):
        at = slice(begin, begin + chunk)
        position = lax.broadcasted_iota(jnp.int32, (1, chunk), 1) + begin
        time = position.astype(F32) * (1.0 / row_len)
        step = lax.rem(
            (lax.broadcasted_iota(jnp.int32, (bands, chunk), 1) + begin) * column,
            jnp.int32(row_len),
        ) if row_len & (row_len - 1) else (
            (lax.broadcasted_iota(jnp.int32, (bands, chunk), 1) + begin) * column & (row_len - 1)
        )
        sin_v, cos_v = sine_cosine(step, row_len)
        embed_ref[0:bands, at] = sin_v
        embed_ref[bands : 2 * bands, at] = cos_v
        tail = lax.broadcasted_iota(jnp.int32, (depth - 2 * bands, chunk), 0)
        embed_ref[2 * bands : depth, at] = jnp.where(
            tail == 0, time, jnp.where(tail == 1, 1.0, 0.0)
        )
        first = sine(dot(w_first, embed_ref[:, at], high))
        second = sine(dot(w_second, first, high))
        shaped = dot(w_last, second, high) * jnp.exp(-rate * time)
        shaped_ref[:, at] = shaped
        energy = energy + jnp.sum(shaped * shaped, axis=1, keepdims=True)
    scale = lax.rsqrt(energy + 1e-06)
    first_lag = lax.broadcasted_iota(jnp.int32, (own, q), 1) == 0
    rows = [shaped_ref[:, d * q : (d + 1) * q] * scale for d in range(blocks)]
    rows[0] = rows[0] + jnp.where(first_lag, direct, 0.0)
    rows = jnp.concatenate(rows, axis=0)
    spec_ref[...] = dot3(rows, fh_ref[...], fl_ref[...])
    sign = (1 - 2 * (lax.broadcasted_iota(jnp.int32, (own, q), 1) & 1)).astype(F32)
    for d in range(blocks):
        here = slice(d * own, (d + 1) * own)
        re = sign * spec_ref[here, q : 2 * q]
        im = -sign * spec_ref[here, 0:q]
        if d:
            before = slice((d - 1) * own, d * own)
            re = re + spec_ref[before, 0:q]
            im = im + spec_ref[before, q : 2 * q]
        g_ref[here, 0:q] = re
        g_ref[here, q : 2 * q] = im - re
        g_ref[here, 2 * q : 3 * q] = re + im


def conv_kernel(q, own, x_ref, g_ref, fh_ref, fl_ref, ih_ref, il_ref, o_ref, spec_ref, prod_ref):
    blocks = x_ref.shape[0] // own
    groups, lanes, pair = own // 8, 128, 2
    for h in range(groups):
        rows = [x_ref[b * own + h * 8 : b * own + h * 8 + 8, :] for b in range(blocks)]
        x = jnp.concatenate(rows, axis=0).astype(BF16)
        re = dot(x, fh_ref[:, 0:q]) + dot(x, fl_ref[:, 0:q])
        im = dot(x, fh_ref[:, q : 2 * q]) + dot(x, fl_ref[:, q : 2 * q])
        at = slice(h * blocks * 8, (h + 1) * blocks * 8)
        spec_ref[at, 0:q] = re
        spec_ref[at, q : 2 * q] = im
        spec_ref[at, 2 * q : 3 * q] = re + im
    for h in range(groups):
        here = [slice((h * blocks + b) * 8, (h * blocks + b + 1) * 8) for b in range(blocks)]
        there = [slice(b * own + h * 8, b * own + h * 8 + 8) for b in range(blocks)]
        for c in range(0, q, lanes):
            planes = [slice(p * q + c, p * q + c + lanes) for p in range(3)]
            for begin in range(0, blocks, pair):
                total = {}
                for a in range(begin + pair):
                    x_re, x_im, x_sum = (spec_ref[here[a], p] for p in planes)
                    for b in range(max(begin, a), begin + pair):
                        g_re, g_diff, g_sum = (g_ref[there[b - a], p] for p in planes)
                        terms = (g_re * x_sum, g_diff * x_re, g_sum * x_im)
                        total[b] = [t + u for t, u in zip(total[b], terms)] if b in total else terms
                for b in range(begin, begin + pair):
                    both, up, down = total[b]
                    prod_ref[here[b], planes[0]] = both - down
                    prod_ref[here[b], planes[1]] = both + up
        y = dot3(prod_ref[h * blocks * 8 : (h + 1) * blocks * 8, :], ih_ref[...], il_ref[...])
        for b in range(blocks):
            o_ref[there[b], :] = y[b * 8 : (b + 1) * 8, :]


def finish_kernel(start_ref, len_ref, conv_ref, gate_ref, o_ref):
    rows, channels = gate_ref.shape
    room = len_ref[0] - start_ref[0]
    live = lax.broadcasted_iota(jnp.int32, (rows, channels), 0) < room
    result = gate_ref[...].astype(F32) * conv_ref[...].T
    o_ref[...] = jnp.where(live, result, 0.0).astype(BF16)


def call(body, out, smem, vmem, scratch=(), flops=0, moved=0, **kwargs):
    return pl.pallas_call(
        body,
        out_shape=out,
        in_specs=[pl.BlockSpec(memory_space=pltpu.SMEM)] * smem
        + [pl.BlockSpec(memory_space=pltpu.VMEM)] * vmem,
        out_specs=pl.BlockSpec(memory_space=pltpu.VMEM),
        scratch_shapes=list(scratch),
        compiler_params=pltpu.CompilerParams(vmem_limit_bytes=VMEM_LIMIT),
        cost_estimate=pl.CostEstimate(flops=flops, bytes_accessed=moved, transcendentals=0),
        **kwargs,
    )


def on_device(values, gate, lengths, bands, w_in, b_in, w_mid, w_out, decay, skip):
    seq_count = lax.axis_size("seq")
    seq_pos = lax.axis_index("seq")
    q, channels = values.shape[1:]
    own = channels // seq_count
    row_len = q * seq_count
    hid = w_mid.shape[0]
    start = (seq_pos * q).astype(jnp.int32).reshape(1)
    first_channel = (seq_pos * own).astype(jnp.int32).reshape(1)
    fh, fl, ih, il = (jnp.asarray(t) for t in dft_tables(q))

    outgoing = turned_live(values[0], seq_count, lengths[0] - start[0])
    incoming = lax.all_to_all(
        outgoing, "seq", split_axis=0, concat_axis=0, tiled=True
    ).reshape(channels, q)

    depth = -(-(w_in.shape[0] + 1) // 8) * 8
    spectrum = call(
        functools.partial(filter_kernel, row_len, q, own),
        jax.ShapeDtypeStruct((channels, 3 * q), F32),
        2,
        8,
        scratch=[
            pltpu.VMEM((128, 128), F32),
            pltpu.VMEM((channels, 128), F32),
            pltpu.VMEM((depth, row_len), F32),
            pltpu.VMEM((own, row_len), F32),
            pltpu.VMEM((channels, 2 * q), F32),
        ],
        flops=6 * 2 * row_len * hid * 256 * 8,
        moved=4 * channels * 2 * q,
    )(first_channel, bands, w_in, b_in.reshape(1, hid), w_mid, w_out, decay.reshape(1, channels),
      skip.reshape(1, channels), fh, fl)

    convolved = call(
        functools.partial(conv_kernel, q, own),
        jax.ShapeDtypeStruct((channels, q), F32),
        0,
        6,
        scratch=[pltpu.VMEM((channels, 3 * q), F32), pltpu.VMEM((channels, 2 * q), F32)],
        flops=5 * 4 * channels * q * q,
        moved=16 * channels * q,
    )(incoming, spectrum, fh, fl, ih, il)
    returned = lax.all_to_all(
        convolved.reshape(seq_count, own, q), "seq", split_axis=0, concat_axis=0, tiled=True
    ).reshape(channels, q)
    return call(
        finish_kernel, jax.ShapeDtypeStruct((q, channels), BF16), 2, 2, moved=8 * q * channels
    )(start, lengths, returned, gate[0])[None]


def solution(mesh):
    split_spec = P("grp", "seq", None)
    return jax.shard_map(
        on_device,
        mesh=mesh,
        in_specs=(split_spec, split_spec, P("grp")) + (P(),) * 7,
        out_specs=split_spec,
        check_vma=False,
    )
```

```python
import functools
import math

import jax
import jax.numpy as jnp
import ml_dtypes
import numpy as np
from jax import lax
from jax.experimental import pallas as pl
from jax.experimental.pallas import tpu as pltpu
from jax.sharding import PartitionSpec as P

F32 = jnp.float32
BF16 = jnp.bfloat16
VMEM_LIMIT = 48 * 1024 * 1024


def split_np(table):
    high = table.astype(np.float32).astype(ml_dtypes.bfloat16)
    low = (table - high.astype(np.float64)).astype(np.float32).astype(ml_dtypes.bfloat16)
    return high, low


def dft_tables(q):
    f = np.arange(q)[None, :]
    n = np.arange(q)[:, None]
    turn = 2.0 * math.pi / (4 * q)
    ahead = ((2 * f + 1) * n % (4 * q)) * turn
    forward = np.concatenate([np.cos(ahead), -np.sin(ahead)], axis=1)
    back = ((2 * f.T + 1) * (n.T + q) % (4 * q)) * turn
    inverse = np.concatenate([np.cos(back), -np.sin(back)], axis=0) / q
    return split_np(forward) + split_np(inverse)


def split(x):
    high = x.astype(BF16)
    return high, (x - high.astype(F32)).astype(BF16)


def dot(a, b, precision=None):
    return lax.dot_general(
        a, b, (((1,), (0,)), ((), ())), precision=precision, preferred_element_type=F32
    )


def dot3(a, b_high, b_low):
    a_high, a_low = split(a)
    return dot(a_high, b_high) + dot(a_low, b_high) + dot(a_high, b_low)


PI_A = 3.140625
PI_B = 9.67502593994140625e-4
PI_C = math.pi - PI_A - PI_B


def odd_fit(func, reach, terms):
    nodes = np.cos(np.pi * (np.arange(400) + 0.5) / 400) * reach
    nodes = nodes[nodes > 0]
    basis = np.stack([nodes ** (2 * i + 1) for i in range(terms)], axis=1)
    weight = 1.0 / nodes[:, None] ** 0.5
    return np.linalg.lstsq(basis * weight, func(nodes) * weight[:, 0], rcond=None)[0]


def even_fit(func, reach, terms):
    nodes = np.cos(np.pi * (np.arange(400) + 0.5) / 400) * reach
    basis = np.stack([nodes ** (2 * i) for i in range(terms)], axis=1)
    return np.linalg.lstsq(basis, func(nodes), rcond=None)[0]


SIN_HALF = [float(c) for c in odd_fit(np.sin, math.pi / 2, 6)]
SIN_QUARTER = [float(c) for c in odd_fit(np.sin, math.pi / 4, 4)]
COS_QUARTER = [float(c) for c in even_fit(np.cos, math.pi / 4, 5)]


def horner(square, coefficients):
    total = jnp.full_like(square, coefficients[-1])
    for c in coefficients[-2::-1]:
        total = total * square + c
    return total


def sine(x):
    turns = lax.round(x * (1.0 / math.pi), lax.RoundingMethod.TO_NEAREST_EVEN)
    r = ((x - turns * PI_A) - turns * PI_B) - turns * PI_C
    value = r * horner(r * r, SIN_HALF)
    odd = (turns.astype(jnp.int32) & 1) == 1
    return jnp.where(odd, -value, value)


def sine_cosine(step, row_len):
    quarter = row_len // 4
    corner = (step + quarter // 2) // quarter
    r = (step - corner * quarter).astype(F32) * (2.0 * math.pi / row_len)
    square = r * r
    s = r * horner(square, SIN_QUARTER)
    c = horner(square, COS_QUARTER)
    swap = (corner & 1) == 1
    sin_v = jnp.where(swap, c, s)
    cos_v = jnp.where(swap, s, c)
    sin_v = jnp.where((corner & 2) == 2, -sin_v, sin_v)
    cos_v = jnp.where(((corner + 1) & 2) == 2, -cos_v, cos_v)
    return sin_v, cos_v


def turn_kernel(parts, x_ref, o_ref, in_ref, out_ref, in_sem, out_sem):
    each = x_ref.shape[1] // parts
    at = [slice(p * each, (p + 1) * each) for p in range(parts)]
    loads = [
        pltpu.make_async_copy(x_ref.at[:, at[p]], in_ref.at[:, at[p]], in_sem.at[p])
        for p in range(parts)
    ]
    stores = [
        pltpu.make_async_copy(out_ref.at[at[p], :], o_ref.at[at[p], :], out_sem.at[p])
        for p in range(parts)
    ]
    for load in loads:
        load.start()
    for p in range(parts):
        loads[p].wait()
        out_ref[at[p], :] = in_ref[:, at[p]].T.astype(F32)
        stores[p].start()
    for store in stores:
        store.wait()


def filter_kernel(
    row_len, q, own, start_ref, len_ref, bands_ref, w_in_ref, b_in_ref, w_mid_ref, w_out_ref, decay_ref,
    skip_ref, fh_ref, fl_ref, g_ref, live_ref, wide_ref, turned_ref, embed_ref, shaped_ref, spec_ref,
):
    hid = w_mid_ref.shape[0]
    bands = bands_ref.shape[0]
    emb = w_in_ref.shape[0]
    channels = w_out_ref.shape[1]
    blocks = row_len // q
    high = lax.Precision.HIGHEST
    spot = lax.broadcasted_iota(jnp.int32, (blocks, q), 0) * q
    spot = spot + lax.broadcasted_iota(jnp.int32, (blocks, q), 1)
    live_ref[...] = jnp.where(spot < len_ref[0], 1.0, 0.0)
    depth = embed_ref.shape[0]

    wide_ref[...] = jnp.zeros_like(wide_ref)
    wide_ref[0 : 2 * bands, 0:hid] = w_in_ref[1:emb, :]
    wide_ref[2 * bands : 2 * bands + 1, 0:hid] = w_in_ref[0:1, :]
    wide_ref[2 * bands + 1 : 2 * bands + 2, 0:hid] = b_in_ref[...]
    w_first = wide_ref[...].T[0:hid, 0:depth]
    wide_ref[...] = jnp.zeros_like(wide_ref)
    wide_ref[0:hid, 0:hid] = w_mid_ref[...]
    w_second = wide_ref[...].T[0:hid, 0:hid]
    turned_ref[:, 0:hid] = w_out_ref[...].T
    turned_ref[:, hid : hid + 8] = jnp.broadcast_to(decay_ref[...], (8, channels)).T
    turned_ref[:, hid + 8 : hid + 16] = jnp.broadcast_to(skip_ref[...], (8, channels)).T
    mine = pl.ds(pl.multiple_of(start_ref[0], own), own)
    w_last = turned_ref[mine, 0:hid]
    rate = turned_ref[mine, hid : hid + 1]
    direct = turned_ref[mine, hid + 8 : hid + 9]

    row = lax.broadcasted_iota(jnp.int32, (bands, 128), 0)
    column = jnp.zeros((bands, 128), jnp.int32)
    for k in range(bands):
        column = jnp.where(row == k, bands_ref[k], column)
    column = column[:, 0:1]

    chunk = min(1024, row_len)
    energy = jnp.zeros((own, 1), F32)
    for begin in range(0, row_len, chunk):
        at = slice(begin, begin + chunk)
        position = lax.broadcasted_iota(jnp.int32, (1, chunk), 1) + begin
        time = position.astype(F32) * (1.0 / row_len)
        step = lax.rem(
            (lax.broadcasted_iota(jnp.int32, (bands, chunk), 1) + begin) * column,
            jnp.int32(row_len),
        ) if row_len & (row_len - 1) else (
            (lax.broadcasted_iota(jnp.int32, (bands, chunk), 1) + begin) * column & (row_len - 1)
        )
        sin_v, cos_v = sine_cosine(step, row_len)
        embed_ref[0:bands, at] = sin_v
        embed_ref[bands : 2 * bands, at] = cos_v
        tail = lax.broadcasted_iota(jnp.int32, (depth - 2 * bands, chunk), 0)
        embed_ref[2 * bands : depth, at] = jnp.where(
            tail == 0, time, jnp.where(tail == 1, 1.0, 0.0)
        )
        first = sine(dot(w_first, embed_ref[:, at], high))
        second = sine(dot(w_second, first, high))
        shaped = dot(w_last, second, high) * jnp.exp(-rate * time)
        shaped_ref[:, at] = shaped
        energy = energy + jnp.sum(shaped * shaped, axis=1, keepdims=True)
    scale = lax.rsqrt(energy + 1e-06)
    first_lag = lax.broadcasted_iota(jnp.int32, (own, q), 1) == 0
    rows = [shaped_ref[:, d * q : (d + 1) * q] * scale for d in range(blocks)]
    rows[0] = rows[0] + jnp.where(first_lag, direct, 0.0)
    rows = jnp.concatenate(rows, axis=0)
    spec_ref[...] = dot3(rows, fh_ref[...], fl_ref[...])
    sign = (1 - 2 * (lax.broadcasted_iota(jnp.int32, (own, q), 1) & 1)).astype(F32)
    for d in range(blocks):
        here = slice(d * own, (d + 1) * own)
        re = sign * spec_ref[here, q : 2 * q]
        im = -sign * spec_ref[here, 0:q]
        if d:
            before = slice((d - 1) * own, d * own)
            re = re + spec_ref[before, 0:q]
            im = im + spec_ref[before, q : 2 * q]
        g_ref[here, 0:q] = re
        g_ref[here, q : 2 * q] = im - re
        g_ref[here, 2 * q : 3 * q] = re + im


def conv_kernel(q, own, x_ref, live_ref, g_ref, fh_ref, fl_ref, ih_ref, il_ref, o_ref, spec_ref, prod_ref):
    blocks = x_ref.shape[0] // own
    groups, lanes, pair = own // 8, 128, 2

    def forward(h):
        rows = [
            x_ref[b * own + h * 8 : b * own + h * 8 + 8, :] * live_ref[b : b + 1, :]
            for b in range(blocks)
        ]
        x = jnp.concatenate(rows, axis=0).astype(BF16)
        re = dot(x, fh_ref[:, 0:q]) + dot(x, fl_ref[:, 0:q])
        im = dot(x, fh_ref[:, q : 2 * q]) + dot(x, fl_ref[:, q : 2 * q])
        at = slice(h * blocks * 8, (h + 1) * blocks * 8)
        spec_ref[at, 0:q] = re
        spec_ref[at, q : 2 * q] = im
        spec_ref[at, 2 * q : 3 * q] = re + im

    def multiply(h):
        here = [slice((h * blocks + b) * 8, (h * blocks + b + 1) * 8) for b in range(blocks)]
        there = [slice(b * own + h * 8, b * own + h * 8 + 8) for b in range(blocks)]
        for c in range(0, q, lanes):
            planes = [slice(p * q + c, p * q + c + lanes) for p in range(3)]
            for begin in range(0, blocks, pair):
                total = {}
                for a in range(begin + pair):
                    x_re, x_im, x_sum = (spec_ref[here[a], p] for p in planes)
                    for b in range(max(begin, a), begin + pair):
                        g_re, g_diff, g_sum = (g_ref[there[b - a], p] for p in planes)
                        terms = (g_re * x_sum, g_diff * x_re, g_sum * x_im)
                        total[b] = [t + u for t, u in zip(total[b], terms)] if b in total else terms
                for b in range(begin, begin + pair):
                    both, up, down = total[b]
                    prod_ref[here[b], planes[0]] = both - down
                    prod_ref[here[b], planes[1]] = both + up

    def inverse(h):
        y = dot3(prod_ref[h * blocks * 8 : (h + 1) * blocks * 8, :], ih_ref[...], il_ref[...])
        for b in range(blocks):
            o_ref[b * own + h * 8 : b * own + h * 8 + 8, :] = y[b * 8 : (b + 1) * 8, :]

    forward(0)
    for h in range(groups):
        if h + 1 < groups:
            forward(h + 1)
        multiply(h)
        if h:
            inverse(h - 1)
    inverse(groups - 1)


def finish_kernel(parts, pos_ref, live_ref, conv_ref, gate_ref, o_ref, out_ref, sem):
    each = gate_ref.shape[1] // parts
    live = live_ref[pl.ds(pos_ref[0], 1), :] > 0.5
    stores = []
    for p in range(parts):
        at = slice(p * each, (p + 1) * each)
        kept = jnp.where(live, conv_ref[at, :], 0.0).T
        out_ref[:, at] = (gate_ref[:, at].astype(F32) * kept).astype(BF16)
        stores.append(pltpu.make_async_copy(out_ref.at[:, at], o_ref.at[:, at], sem.at[p]))
        stores[p].start()
    for store in stores:
        store.wait()


def call(body, out, smem, vmem, scratch=(), flops=0, moved=0, **kwargs):
    return pl.pallas_call(
        body,
        out_shape=out,
        in_specs=[pl.BlockSpec(memory_space=pltpu.SMEM)] * smem
        + [pl.BlockSpec(memory_space=pltpu.VMEM)] * vmem,
        out_specs=jax.tree.map(lambda _: pl.BlockSpec(memory_space=pltpu.VMEM), out),
        scratch_shapes=list(scratch),
        compiler_params=pltpu.CompilerParams(vmem_limit_bytes=VMEM_LIMIT),
        cost_estimate=pl.CostEstimate(flops=flops, bytes_accessed=moved, transcendentals=0),
        **kwargs,
    )


def on_device(values, gate, lengths, bands, w_in, b_in, w_mid, w_out, decay, skip):
    seq_count = lax.axis_size("seq")
    seq_pos = lax.axis_index("seq")
    q, channels = values.shape[1:]
    own = channels // seq_count
    row_len = q * seq_count
    hid = w_mid.shape[0]
    first_channel = (seq_pos * own).astype(jnp.int32).reshape(1)
    fh, fl, ih, il = (jnp.asarray(t) for t in dft_tables(q))

    parts = 4
    outgoing = pl.pallas_call(
        functools.partial(turn_kernel, parts),
        out_shape=jax.ShapeDtypeStruct((channels, q), F32),
        in_specs=[pl.BlockSpec(memory_space=pltpu.HBM)],
        out_specs=pl.BlockSpec(memory_space=pl.ANY),
        scratch_shapes=[
            pltpu.VMEM((q, channels), BF16),
            pltpu.VMEM((channels, q), F32),
            pltpu.SemaphoreType.DMA((parts,)),
            pltpu.SemaphoreType.DMA((parts,)),
        ],
        compiler_params=pltpu.CompilerParams(vmem_limit_bytes=8 * 1024 * 1024),
        cost_estimate=pl.CostEstimate(flops=0, bytes_accessed=6 * q * channels, transcendentals=0),
    )(pltpu.with_memory_space_constraint(values[0], pltpu.HBM))
    incoming = lax.all_to_all(
        outgoing.reshape(seq_count, own, q), "seq", split_axis=0, concat_axis=0, tiled=True
    ).reshape(channels, q)

    depth = -(-(w_in.shape[0] + 1) // 8) * 8
    spectrum, live = call(
        functools.partial(filter_kernel, row_len, q, own),
        [
            jax.ShapeDtypeStruct((channels, 3 * q), F32),
            jax.ShapeDtypeStruct((seq_count, q), F32),
        ],
        3,
        8,
        scratch=[
            pltpu.VMEM((128, 128), F32),
            pltpu.VMEM((channels, 128), F32),
            pltpu.VMEM((depth, row_len), F32),
            pltpu.VMEM((own, row_len), F32),
            pltpu.VMEM((channels, 2 * q), F32),
        ],
        flops=6 * 2 * row_len * hid * 256 * 8,
        moved=4 * channels * 2 * q,
    )(first_channel, lengths, bands, w_in, b_in.reshape(1, hid), w_mid, w_out, decay.reshape(1, channels),
      skip.reshape(1, channels), fh, fl)

    convolved = call(
        functools.partial(conv_kernel, q, own),
        jax.ShapeDtypeStruct((channels, q), F32),
        0,
        7,
        scratch=[pltpu.VMEM((channels, 3 * q), F32), pltpu.VMEM((channels, 2 * q), F32)],
        flops=5 * 4 * channels * q * q,
        moved=16 * channels * q,
    )(incoming, live, spectrum, fh, fl, ih, il)
    returned = lax.all_to_all(
        convolved.reshape(seq_count, own, q), "seq", split_axis=0, concat_axis=0, tiled=True
    ).reshape(channels, q)
    halves = 2
    return pl.pallas_call(
        functools.partial(finish_kernel, halves),
        out_shape=jax.ShapeDtypeStruct((q, channels), BF16),
        in_specs=[pl.BlockSpec(memory_space=pltpu.SMEM)]
        + [pl.BlockSpec(memory_space=pltpu.VMEM)] * 3,
        out_specs=pl.BlockSpec(memory_space=pl.ANY),
        scratch_shapes=[pltpu.VMEM((q, channels), BF16), pltpu.SemaphoreType.DMA((halves,))],
        compiler_params=pltpu.CompilerParams(vmem_limit_bytes=8 * 1024 * 1024),
        cost_estimate=pl.CostEstimate(flops=0, bytes_accessed=8 * q * channels, transcendentals=0),
    )(seq_pos.astype(jnp.int32).reshape(1), live, returned, gate[0])[None]


def solution(mesh):
    split_spec = P("grp", "seq", None)
    return jax.shard_map(
        on_device,
        mesh=mesh,
        in_specs=(split_spec, split_spec, P("grp")) + (P(),) * 7,
        out_specs=split_spec,
        check_vma=False,
    )
```

```python
import functools
import math

import jax
import jax.numpy as jnp
import ml_dtypes
import numpy as np
from jax import lax
from jax.experimental import pallas as pl
from jax.experimental.pallas import tpu as pltpu
from jax.sharding import PartitionSpec as P

F32 = jnp.float32
BF16 = jnp.bfloat16
VMEM_LIMIT = 20 * 1024 * 1024


def split_np(table):
    high = table.astype(np.float32).astype(ml_dtypes.bfloat16)
    low = (table - high.astype(np.float64)).astype(np.float32).astype(ml_dtypes.bfloat16)
    return high, low


def dft_tables(q):
    f = np.arange(q)[None, :]
    n = np.arange(q)[:, None]
    turn = 2.0 * math.pi / (4 * q)
    ahead = ((2 * f + 1) * n % (4 * q)) * turn
    forward = np.concatenate([np.cos(ahead), -np.sin(ahead)], axis=1)
    back = ((2 * f.T + 1) * (n.T + q) % (4 * q)) * turn
    inverse = np.concatenate([np.cos(back), -np.sin(back)], axis=0) / q
    return np.concatenate(
        [*split_np(forward), np.concatenate(split_np(inverse), axis=1)], axis=0
    )


def split(x):
    high = x.astype(BF16)
    return high, (x - high.astype(F32)).astype(BF16)


def dot(a, b, precision=None):
    return lax.dot_general(
        a, b, (((1,), (0,)), ((), ())), precision=precision, preferred_element_type=F32
    )


def dot3(a, b_high, b_low):
    a_high, a_low = split(a)
    return dot(a_high, b_high) + dot(a_low, b_high) + dot(a_high, b_low)


PI_A = 3.140625
PI_B = 9.67502593994140625e-4
PI_C = math.pi - PI_A - PI_B


def odd_fit(func, reach, terms):
    nodes = np.cos(np.pi * (np.arange(400) + 0.5) / 400) * reach
    nodes = nodes[nodes > 0]
    basis = np.stack([nodes ** (2 * i + 1) for i in range(terms)], axis=1)
    weight = 1.0 / nodes[:, None] ** 0.5
    return np.linalg.lstsq(basis * weight, func(nodes) * weight[:, 0], rcond=None)[0]


def even_fit(func, reach, terms):
    nodes = np.cos(np.pi * (np.arange(400) + 0.5) / 400) * reach
    basis = np.stack([nodes ** (2 * i) for i in range(terms)], axis=1)
    return np.linalg.lstsq(basis, func(nodes), rcond=None)[0]


SIN_HALF = [float(c) for c in odd_fit(np.sin, math.pi / 2, 6)]
SIN_QUARTER = [float(c) for c in odd_fit(np.sin, math.pi / 4, 4)]
COS_QUARTER = [float(c) for c in even_fit(np.cos, math.pi / 4, 5)]


def horner(square, coefficients):
    total = jnp.full_like(square, coefficients[-1])
    for c in coefficients[-2::-1]:
        total = total * square + c
    return total


def sine(x):
    turns = lax.round(x * (1.0 / math.pi), lax.RoundingMethod.TO_NEAREST_EVEN)
    r = ((x - turns * PI_A) - turns * PI_B) - turns * PI_C
    value = r * horner(r * r, SIN_HALF)
    odd = (turns.astype(jnp.int32) & 1) == 1
    return jnp.where(odd, -value, value)


def sine_cosine(step, row_len):
    quarter = row_len // 4
    corner = (step + quarter // 2) // quarter
    r = (step - corner * quarter).astype(F32) * (2.0 * math.pi / row_len)
    square = r * r
    s = r * horner(square, SIN_QUARTER)
    c = horner(square, COS_QUARTER)
    swap = (corner & 1) == 1
    sin_v = jnp.where(swap, c, s)
    cos_v = jnp.where(swap, s, c)
    sin_v = jnp.where((corner & 2) == 2, -sin_v, sin_v)
    cos_v = jnp.where(((corner + 1) & 2) == 2, -cos_v, cos_v)
    return sin_v, cos_v


def turn_kernel(parts, x_ref, o_ref, in_ref, out_ref, in_sem, out_sem):
    each = x_ref.shape[1] // parts
    at = [slice(p * each, (p + 1) * each) for p in range(parts)]
    loads = [
        pltpu.make_async_copy(x_ref.at[:, at[p]], in_ref.at[:, at[p]], in_sem.at[p])
        for p in range(parts)
    ]
    stores = [
        pltpu.make_async_copy(out_ref.at[at[p], :], o_ref.at[at[p], :], out_sem.at[p])
        for p in range(parts)
    ]
    for load in loads:
        load.start()
    for p in range(parts):
        loads[p].wait()
        out_ref[at[p], :] = in_ref[:, at[p]].T.astype(F32)
        stores[p].start()
    for store in stores:
        store.wait()


def filter_kernel(
    row_len, q, own, start_ref, len_ref, bands_ref, w_in_ref, b_in_ref, w_mid_ref, w_out_ref, decay_ref,
    skip_ref, gate_ref, table_ref, g_ref, live_ref, turned_gate_ref, wide_ref, turned_ref, embed_ref, shaped_ref, spec_ref,
):
    hid = w_mid_ref.shape[0]
    bands = bands_ref.shape[0]
    emb = w_in_ref.shape[0]
    channels = w_out_ref.shape[1]
    blocks = row_len // q
    high = lax.Precision.HIGHEST
    spot = lax.broadcasted_iota(jnp.int32, (blocks, q), 0) * q
    spot = spot + lax.broadcasted_iota(jnp.int32, (blocks, q), 1)
    live_ref[...] = jnp.where(spot < len_ref[0], 1.0, 0.0)
    room = len_ref[0] - lax.div(start_ref[0] * q, jnp.int32(own))
    here_live = lax.broadcasted_iota(jnp.int32, (1, q), 1) < room
    turned_gate_ref[...] = jnp.where(here_live, gate_ref[...].T.astype(F32), 0.0)
    depth = embed_ref.shape[0]

    wide_ref[...] = jnp.zeros_like(wide_ref)
    wide_ref[0 : 2 * bands, 0:hid] = w_in_ref[1:emb, :]
    wide_ref[2 * bands : 2 * bands + 1, 0:hid] = w_in_ref[0:1, :]
    wide_ref[2 * bands + 1 : 2 * bands + 2, 0:hid] = b_in_ref[...]
    w_first = wide_ref[...].T[0:hid, 0:depth]
    wide_ref[...] = jnp.zeros_like(wide_ref)
    wide_ref[0:hid, 0:hid] = w_mid_ref[...]
    w_second = wide_ref[...].T[0:hid, 0:hid]
    turned_ref[:, 0:hid] = w_out_ref[...].T
    turned_ref[:, hid : hid + 8] = jnp.broadcast_to(decay_ref[...], (8, channels)).T
    turned_ref[:, hid + 8 : hid + 16] = jnp.broadcast_to(skip_ref[...], (8, channels)).T
    mine = pl.ds(pl.multiple_of(start_ref[0], own), own)
    w_last = turned_ref[mine, 0:hid]
    rate = turned_ref[mine, hid : hid + 1]
    direct = turned_ref[mine, hid + 8 : hid + 9]

    row = lax.broadcasted_iota(jnp.int32, (bands, 128), 0)
    column = jnp.zeros((bands, 128), jnp.int32)
    for k in range(bands):
        column = jnp.where(row == k, bands_ref[k], column)
    column = column[:, 0:1]

    chunk = min(1024, row_len)
    energy = jnp.zeros((own, 1), F32)
    for begin in range(0, row_len, chunk):
        at = slice(begin, begin + chunk)
        position = lax.broadcasted_iota(jnp.int32, (1, chunk), 1) + begin
        time = position.astype(F32) * (1.0 / row_len)
        step = lax.rem(
            (lax.broadcasted_iota(jnp.int32, (bands, chunk), 1) + begin) * column,
            jnp.int32(row_len),
        ) if row_len & (row_len - 1) else (
            (lax.broadcasted_iota(jnp.int32, (bands, chunk), 1) + begin) * column & (row_len - 1)
        )
        sin_v, cos_v = sine_cosine(step, row_len)
        embed_ref[0:bands, at] = sin_v
        embed_ref[bands : 2 * bands, at] = cos_v
        tail = lax.broadcasted_iota(jnp.int32, (depth - 2 * bands, chunk), 0)
        embed_ref[2 * bands : depth, at] = jnp.where(
            tail == 0, time, jnp.where(tail == 1, 1.0, 0.0)
        )
        first = sine(dot(w_first, embed_ref[:, at], high))
        second = sine(dot(w_second, first, high))
        shaped = dot(w_last, second, high) * jnp.exp(-rate * time)
        shaped_ref[:, at] = shaped
        energy = energy + jnp.sum(shaped * shaped, axis=1, keepdims=True)
    scale = lax.rsqrt(energy + 1e-06)
    first_lag = lax.broadcasted_iota(jnp.int32, (own, q), 1) == 0
    rows = [shaped_ref[:, d * q : (d + 1) * q] * scale for d in range(blocks)]
    rows[0] = rows[0] + jnp.where(first_lag, direct, 0.0)
    rows = jnp.concatenate(rows, axis=0)
    spec_ref[...] = dot3(rows, table_ref[0:q, :], table_ref[q : 2 * q, :])
    sign = (1 - 2 * (lax.broadcasted_iota(jnp.int32, (own, q), 1) & 1)).astype(F32)
    for d in range(blocks):
        here = slice(d * own, (d + 1) * own)
        re = sign * spec_ref[here, q : 2 * q]
        im = -sign * spec_ref[here, 0:q]
        if d:
            before = slice((d - 1) * own, d * own)
            re = re + spec_ref[before, 0:q]
            im = im + spec_ref[before, q : 2 * q]
        g_ref[here, 0:q] = re
        g_ref[here, q : 2 * q] = im - re
        g_ref[here, 2 * q : 3 * q] = re + im


def conv_kernel(q, own, x_ref, live_ref, g_ref, table_ref, o_ref, spec_ref, prod_ref):
    blocks = x_ref.shape[0] // own
    groups, lanes, pair = own // 8, 128, 2

    def forward(h):
        rows = [
            x_ref[b * own + h * 8 : b * own + h * 8 + 8, :] * live_ref[b : b + 1, :]
            for b in range(blocks)
        ]
        x = jnp.concatenate(rows, axis=0).astype(BF16)
        high, low = slice(0, q), slice(q, 2 * q)
        re = dot(x, table_ref[high, 0:q]) + dot(x, table_ref[low, 0:q])
        im = dot(x, table_ref[high, q : 2 * q]) + dot(x, table_ref[low, q : 2 * q])
        at = slice(h * blocks * 8, (h + 1) * blocks * 8)
        spec_ref[at, 0:q] = re
        spec_ref[at, q : 2 * q] = im
        spec_ref[at, 2 * q : 3 * q] = re + im

    def multiply(h):
        here = [slice((h * blocks + b) * 8, (h * blocks + b + 1) * 8) for b in range(blocks)]
        there = [slice(b * own + h * 8, b * own + h * 8 + 8) for b in range(blocks)]
        for c in range(0, q, lanes):
            planes = [slice(p * q + c, p * q + c + lanes) for p in range(3)]
            for begin in range(0, blocks, pair):
                total = {}
                for a in range(begin + pair):
                    x_re, x_im, x_sum = (spec_ref[here[a], p] for p in planes)
                    for b in range(max(begin, a), begin + pair):
                        g_re, g_diff, g_sum = (g_ref[there[b - a], p] for p in planes)
                        terms = (g_re * x_sum, g_diff * x_re, g_sum * x_im)
                        total[b] = [t + u for t, u in zip(total[b], terms)] if b in total else terms
                for b in range(begin, begin + pair):
                    both, up, down = total[b]
                    prod_ref[here[b], planes[0]] = both - down
                    prod_ref[here[b], planes[1]] = both + up

    def inverse(h):
        y = dot3(prod_ref[h * blocks * 8 : (h + 1) * blocks * 8, :], table_ref[2 * q : 4 * q, 0:q], table_ref[2 * q : 4 * q, q : 2 * q])
        for b in range(blocks):
            o_ref[b * own + h * 8 : b * own + h * 8 + 8, :] = y[b * 8 : (b + 1) * 8, :]

    forward(0)
    for h in range(groups):
        if h + 1 < groups:
            forward(h + 1)
        multiply(h)
        if h:
            inverse(h - 1)
    inverse(groups - 1)


def finish_kernel(parts, conv_ref, gate_ref, o_ref, out_ref, sem):
    each = gate_ref.shape[0] // parts
    stores = []
    for p in range(parts):
        at = slice(p * each, (p + 1) * each)
        out_ref[:, at] = (conv_ref[at, :] * gate_ref[at, :]).T.astype(BF16)
        stores.append(pltpu.make_async_copy(out_ref.at[:, at], o_ref.at[:, at], sem.at[p]))
        stores[p].start()
    for store in stores:
        store.wait()


def call(body, out, smem, vmem, scratch=(), flops=0, moved=0, **kwargs):
    return pl.pallas_call(
        body,
        out_shape=out,
        in_specs=[pl.BlockSpec(memory_space=pltpu.SMEM)] * smem
        + [pl.BlockSpec(memory_space=pltpu.VMEM)] * vmem,
        out_specs=jax.tree.map(lambda _: pl.BlockSpec(memory_space=pltpu.VMEM), out),
        scratch_shapes=list(scratch),
        compiler_params=pltpu.CompilerParams(vmem_limit_bytes=VMEM_LIMIT),
        cost_estimate=pl.CostEstimate(flops=flops, bytes_accessed=moved, transcendentals=0),
        **kwargs,
    )


def on_device(values, gate, lengths, bands, w_in, b_in, w_mid, w_out, decay, skip):
    seq_count = lax.axis_size("seq")
    seq_pos = lax.axis_index("seq")
    q, channels = values.shape[1:]
    own = channels // seq_count
    row_len = q * seq_count
    hid = w_mid.shape[0]
    first_channel = (seq_pos * own).astype(jnp.int32).reshape(1)
    table = jnp.asarray(dft_tables(q))

    parts = 4
    outgoing = pl.pallas_call(
        functools.partial(turn_kernel, parts),
        out_shape=jax.ShapeDtypeStruct((channels, q), F32),
        in_specs=[pl.BlockSpec(memory_space=pltpu.HBM)],
        out_specs=pl.BlockSpec(memory_space=pl.ANY),
        scratch_shapes=[
            pltpu.VMEM((q, channels), BF16),
            pltpu.VMEM((channels, q), F32),
            pltpu.SemaphoreType.DMA((parts,)),
            pltpu.SemaphoreType.DMA((parts,)),
        ],
        compiler_params=pltpu.CompilerParams(vmem_limit_bytes=8 * 1024 * 1024),
        cost_estimate=pl.CostEstimate(flops=0, bytes_accessed=6 * q * channels, transcendentals=0),
    )(pltpu.with_memory_space_constraint(values[0], pltpu.HBM))
    incoming = lax.all_to_all(
        outgoing.reshape(seq_count, own, q), "seq", split_axis=0, concat_axis=0, tiled=True
    ).reshape(channels, q)

    depth = -(-(w_in.shape[0] + 1) // 8) * 8
    spectrum, live, turned_gate = call(
        functools.partial(filter_kernel, row_len, q, own),
        [
            jax.ShapeDtypeStruct((channels, 3 * q), F32),
            jax.ShapeDtypeStruct((seq_count, q), F32),
            jax.ShapeDtypeStruct((channels, q), F32),
        ],
        3,
        8,
        scratch=[
            pltpu.VMEM((128, 128), F32),
            pltpu.VMEM((channels, 128), F32),
            pltpu.VMEM((depth, row_len), F32),
            pltpu.VMEM((own, row_len), F32),
            pltpu.VMEM((channels, 2 * q), F32),
        ],
        flops=6 * 2 * row_len * hid * 256 * 8,
        moved=4 * channels * 2 * q,
    )(first_channel, lengths, bands, w_in, b_in.reshape(1, hid), w_mid, w_out, decay.reshape(1, channels),
      skip.reshape(1, channels), gate[0], table)

    convolved = call(
        functools.partial(conv_kernel, q, own),
        jax.ShapeDtypeStruct((channels, q), F32),
        0,
        4,
        scratch=[pltpu.VMEM((channels, 3 * q), F32), pltpu.VMEM((channels, 2 * q), F32)],
        flops=5 * 4 * channels * q * q,
        moved=16 * channels * q,
    )(incoming, live, spectrum, table)
    returned = lax.all_to_all(
        convolved.reshape(seq_count, own, q), "seq", split_axis=0, concat_axis=0, tiled=True
    ).reshape(channels, q)
    halves = 2
    return pl.pallas_call(
        functools.partial(finish_kernel, halves),
        out_shape=jax.ShapeDtypeStruct((q, channels), BF16),
        in_specs=[pl.BlockSpec(memory_space=pltpu.VMEM)] * 2,
        out_specs=pl.BlockSpec(memory_space=pl.ANY),
        scratch_shapes=[pltpu.VMEM((q, channels), BF16), pltpu.SemaphoreType.DMA((halves,))],
        compiler_params=pltpu.CompilerParams(vmem_limit_bytes=8 * 1024 * 1024),
        cost_estimate=pl.CostEstimate(flops=0, bytes_accessed=8 * q * channels, transcendentals=0),
    )(returned, turned_gate)[None]


def solution(mesh):
    split_spec = P("grp", "seq", None)
    return jax.shard_map(
        on_device,
        mesh=mesh,
        in_specs=(split_spec, split_spec, P("grp")) + (P(),) * 7,
        out_specs=split_spec,
        check_vma=False,
    )
```

```python
import functools
import math

import jax
import jax.numpy as jnp
import ml_dtypes
import numpy as np
from jax import lax
from jax.experimental import pallas as pl
from jax.experimental.pallas import tpu as pltpu
from jax.sharding import PartitionSpec as P

F32 = jnp.float32
BF16 = jnp.bfloat16
VMEM_LIMIT = 20 * 1024 * 1024


def split_np(table):
    high = table.astype(np.float32).astype(ml_dtypes.bfloat16)
    low = (table - high.astype(np.float64)).astype(np.float32).astype(ml_dtypes.bfloat16)
    return high, low


def dft_tables(q):
    f = np.arange(q)[None, :]
    n = np.arange(q)[:, None]
    turn = 2.0 * math.pi / (4 * q)
    ahead = ((2 * f + 1) * n % (4 * q)) * turn
    forward = np.concatenate([np.cos(ahead), -np.sin(ahead)], axis=1)
    back = ((2 * f.T + 1) * (n.T + q) % (4 * q)) * turn
    inverse = np.concatenate([np.cos(back), -np.sin(back)], axis=0) / q
    return np.concatenate(
        [*split_np(forward), np.concatenate(split_np(inverse), axis=1)], axis=0
    )


def split(x):
    high = x.astype(BF16)
    return high, (x - high.astype(F32)).astype(BF16)


def dot(a, b, precision=None):
    return lax.dot_general(
        a, b, (((1,), (0,)), ((), ())), precision=precision, preferred_element_type=F32
    )


def dot3(a, b_high, b_low):
    a_high, a_low = split(a)
    return dot(a_high, b_high) + dot(a_low, b_high) + dot(a_high, b_low)


PI_A = 3.140625
PI_B = 9.67502593994140625e-4
PI_C = math.pi - PI_A - PI_B


def odd_fit(func, reach, terms):
    nodes = np.cos(np.pi * (np.arange(400) + 0.5) / 400) * reach
    nodes = nodes[nodes > 0]
    basis = np.stack([nodes ** (2 * i + 1) for i in range(terms)], axis=1)
    weight = 1.0 / nodes[:, None] ** 0.5
    return np.linalg.lstsq(basis * weight, func(nodes) * weight[:, 0], rcond=None)[0]


def even_fit(func, reach, terms):
    nodes = np.cos(np.pi * (np.arange(400) + 0.5) / 400) * reach
    basis = np.stack([nodes ** (2 * i) for i in range(terms)], axis=1)
    return np.linalg.lstsq(basis, func(nodes), rcond=None)[0]


SIN_HALF = [float(c) for c in odd_fit(np.sin, math.pi / 2, 6)]
SIN_QUARTER = [float(c) for c in odd_fit(np.sin, math.pi / 4, 4)]
COS_QUARTER = [float(c) for c in even_fit(np.cos, math.pi / 4, 5)]


def horner(square, coefficients):
    total = jnp.full_like(square, coefficients[-1])
    for c in coefficients[-2::-1]:
        total = total * square + c
    return total


def sine(x):
    turns = lax.round(x * (1.0 / math.pi), lax.RoundingMethod.TO_NEAREST_EVEN)
    r = ((x - turns * PI_A) - turns * PI_B) - turns * PI_C
    value = r * horner(r * r, SIN_HALF)
    odd = (turns.astype(jnp.int32) & 1) == 1
    return jnp.where(odd, -value, value)


def sine_cosine(step, row_len):
    quarter = row_len // 4
    corner = (step + quarter // 2) // quarter
    r = (step - corner * quarter).astype(F32) * (2.0 * math.pi / row_len)
    square = r * r
    s = r * horner(square, SIN_QUARTER)
    c = horner(square, COS_QUARTER)
    swap = (corner & 1) == 1
    sin_v = jnp.where(swap, c, s)
    cos_v = jnp.where(swap, s, c)
    sin_v = jnp.where((corner & 2) == 2, -sin_v, sin_v)
    cos_v = jnp.where(((corner + 1) & 2) == 2, -cos_v, cos_v)
    return sin_v, cos_v


def turn_kernel(parts, x_ref, o_ref, in_ref, out_ref, in_sem, out_sem):
    each = x_ref.shape[1] // parts
    at = [slice(p * each, (p + 1) * each) for p in range(parts)]
    loads = [
        pltpu.make_async_copy(x_ref.at[:, at[p]], in_ref.at[:, at[p]], in_sem.at[p])
        for p in range(parts)
    ]
    stores = [
        pltpu.make_async_copy(out_ref.at[at[p], :], o_ref.at[at[p], :], out_sem.at[p])
        for p in range(parts)
    ]
    for load in loads:
        load.start()
    for p in range(parts):
        loads[p].wait()
        out_ref[at[p], :] = in_ref[:, at[p]].T.astype(F32)
        stores[p].start()
    for store in stores:
        store.wait()


def filter_kernel(
    row_len, q, own, start_ref, len_ref, bands_ref, w_in_ref, b_in_ref, w_mid_ref, w_out_ref, decay_ref,
    skip_ref, gate_ref, table_ref, g_ref, live_ref, turned_gate_ref, wide_ref, turned_ref, embed_ref, shaped_ref, spec_ref,
):
    hid = w_mid_ref.shape[0]
    bands = bands_ref.shape[0]
    emb = w_in_ref.shape[0]
    channels = w_out_ref.shape[1]
    blocks = row_len // q
    high = lax.Precision.HIGHEST
    spot = lax.broadcasted_iota(jnp.int32, (blocks, q), 0) * q
    spot = spot + lax.broadcasted_iota(jnp.int32, (blocks, q), 1)
    live_ref[...] = jnp.where(spot < len_ref[0], 1.0, 0.0)
    room = len_ref[0] - lax.div(start_ref[0] * q, jnp.int32(own))
    here_live = lax.broadcasted_iota(jnp.int32, (1, q), 1) < room
    turned_gate_ref[...] = jnp.where(here_live, gate_ref[...].T.astype(F32), 0.0)
    depth = embed_ref.shape[0]

    wide_ref[...] = jnp.zeros_like(wide_ref)
    wide_ref[0 : 2 * bands, 0:hid] = w_in_ref[1:emb, :]
    wide_ref[2 * bands : 2 * bands + 1, 0:hid] = w_in_ref[0:1, :]
    wide_ref[2 * bands + 1 : 2 * bands + 2, 0:hid] = b_in_ref[...]
    w_first = wide_ref[...].T[0:hid, 0:depth]
    wide_ref[...] = jnp.zeros_like(wide_ref)
    wide_ref[0:hid, 0:hid] = w_mid_ref[...]
    w_second = wide_ref[...].T[0:hid, 0:hid]
    turned_ref[:, 0:hid] = w_out_ref[...].T
    turned_ref[:, hid : hid + 8] = jnp.broadcast_to(decay_ref[...], (8, channels)).T
    turned_ref[:, hid + 8 : hid + 16] = jnp.broadcast_to(skip_ref[...], (8, channels)).T
    mine = pl.ds(pl.multiple_of(start_ref[0], own), own)
    w_last = turned_ref[mine, 0:hid]
    rate = turned_ref[mine, hid : hid + 1]
    direct = turned_ref[mine, hid + 8 : hid + 9]

    row = lax.broadcasted_iota(jnp.int32, (bands, 128), 0)
    column = jnp.zeros((bands, 128), jnp.int32)
    for k in range(bands):
        column = jnp.where(row == k, bands_ref[k], column)
    column = column[:, 0:1]

    chunk = min(1024, row_len)
    energy = jnp.zeros((own, 1), F32)
    for begin in range(0, row_len, chunk):
        at = slice(begin, begin + chunk)
        position = lax.broadcasted_iota(jnp.int32, (1, chunk), 1) + begin
        time = position.astype(F32) * (1.0 / row_len)
        step = lax.rem(
            (lax.broadcasted_iota(jnp.int32, (bands, chunk), 1) + begin) * column,
            jnp.int32(row_len),
        ) if row_len & (row_len - 1) else (
            (lax.broadcasted_iota(jnp.int32, (bands, chunk), 1) + begin) * column & (row_len - 1)
        )
        sin_v, cos_v = sine_cosine(step, row_len)
        embed_ref[0:bands, at] = sin_v
        embed_ref[bands : 2 * bands, at] = cos_v
        tail = lax.broadcasted_iota(jnp.int32, (depth - 2 * bands, chunk), 0)
        embed_ref[2 * bands : depth, at] = jnp.where(
            tail == 0, time, jnp.where(tail == 1, 1.0, 0.0)
        )
        first = sine(dot(w_first, embed_ref[:, at], high))
        second = sine(dot(w_second, first, high))
        shaped = dot(w_last, second, high) * jnp.exp(-rate * time)
        shaped_ref[:, at] = shaped
        energy = energy + jnp.sum(shaped * shaped, axis=1, keepdims=True)
    scale = lax.rsqrt(energy + 1e-06)
    first_lag = lax.broadcasted_iota(jnp.int32, (own, q), 1) == 0
    rows = [shaped_ref[:, d * q : (d + 1) * q] * scale for d in range(blocks)]
    rows[0] = rows[0] + jnp.where(first_lag, direct, 0.0)
    rows = jnp.concatenate(rows, axis=0)
    spec_ref[...] = dot3(rows, table_ref[0:q, :], table_ref[q : 2 * q, :])
    sign = (1 - 2 * (lax.broadcasted_iota(jnp.int32, (own, q), 1) & 1)).astype(F32)
    for d in range(blocks):
        here = slice(d * own, (d + 1) * own)
        re = sign * spec_ref[here, q : 2 * q]
        im = -sign * spec_ref[here, 0:q]
        if d:
            before = slice((d - 1) * own, d * own)
            re = re + spec_ref[before, 0:q]
            im = im + spec_ref[before, q : 2 * q]
        g_ref[here, 0:q] = re
        g_ref[here, q : 2 * q] = im - re
        g_ref[here, 2 * q : 3 * q] = re + im


def conv_kernel(q, own, x_ref, live_ref, g_ref, table_ref, o_ref, spec_ref, prod_ref):
    blocks = x_ref.shape[0] // own
    groups, lanes, pair = own // 8, 128, 2

    def forward(h):
        rows = [
            x_ref[b * own + h * 8 : b * own + h * 8 + 8, :] * live_ref[b : b + 1, :]
            for b in range(blocks)
        ]
        x = jnp.concatenate(rows, axis=0).astype(BF16)
        high, low = slice(0, q), slice(q, 2 * q)
        re = dot(x, table_ref[high, 0:q]) + dot(x, table_ref[low, 0:q])
        im = dot(x, table_ref[high, q : 2 * q]) + dot(x, table_ref[low, q : 2 * q])
        at = slice(h * blocks * 8, (h + 1) * blocks * 8)
        spec_ref[at, 0:q] = re
        spec_ref[at, q : 2 * q] = im
        spec_ref[at, 2 * q : 3 * q] = re + im

    def multiply(h):
        here = [slice((h * blocks + b) * 8, (h * blocks + b + 1) * 8) for b in range(blocks)]
        there = [slice(b * own + h * 8, b * own + h * 8 + 8) for b in range(blocks)]
        for c in range(0, q, lanes):
            planes = [slice(p * q + c, p * q + c + lanes) for p in range(3)]
            for begin in range(0, blocks, pair):
                total = {}
                for a in range(begin + pair):
                    x_re, x_im, x_sum = (spec_ref[here[a], p] for p in planes)
                    for b in range(max(begin, a), begin + pair):
                        g_re, g_diff, g_sum = (g_ref[there[b - a], p] for p in planes)
                        terms = (g_re * x_sum, g_diff * x_re, g_sum * x_im)
                        total[b] = [t + u for t, u in zip(total[b], terms)] if b in total else terms
                for b in range(begin, begin + pair):
                    both, up, down = total[b]
                    prod_ref[here[b], planes[0]] = both - down
                    prod_ref[here[b], planes[1]] = both + up

    def inverse(h):
        y = dot3(prod_ref[h * blocks * 8 : (h + 1) * blocks * 8, :], table_ref[2 * q : 4 * q, 0:q], table_ref[2 * q : 4 * q, q : 2 * q])
        for b in range(blocks):
            o_ref[b * own + h * 8 : b * own + h * 8 + 8, :] = y[b * 8 : (b + 1) * 8, :]

    forward(0)
    for h in range(groups):
        if h + 1 < groups:
            forward(h + 1)
        multiply(h)
        if h:
            inverse(h - 1)
    inverse(groups - 1)


def finish_kernel(parts, conv_ref, gate_ref, o_ref, out_ref, sem):
    each = gate_ref.shape[0] // parts
    stores = []
    for p in range(parts):
        at = slice(p * each, (p + 1) * each)
        out_ref[:, at] = (conv_ref[at, :] * gate_ref[at, :]).T.astype(BF16)
        stores.append(pltpu.make_async_copy(out_ref.at[:, at], o_ref.at[:, at], sem.at[p]))
        stores[p].start()
    for store in stores:
        store.wait()


def call(body, out, smem, vmem, scratch=(), flops=0, moved=0, **kwargs):
    return pl.pallas_call(
        body,
        out_shape=out,
        in_specs=[pl.BlockSpec(memory_space=pltpu.SMEM)] * smem
        + [pl.BlockSpec(memory_space=pltpu.VMEM)] * vmem,
        out_specs=jax.tree.map(lambda _: pl.BlockSpec(memory_space=pltpu.VMEM), out),
        scratch_shapes=list(scratch),
        compiler_params=pltpu.CompilerParams(vmem_limit_bytes=VMEM_LIMIT),
        cost_estimate=pl.CostEstimate(flops=flops, bytes_accessed=moved, transcendentals=0),
        **kwargs,
    )


def on_device(values, gate, lengths, bands, w_in, b_in, w_mid, w_out, decay, skip):
    seq_count = lax.axis_size("seq")
    seq_pos = lax.axis_index("seq")
    q, channels = values.shape[1:]
    own = channels // seq_count
    row_len = q * seq_count
    hid = w_mid.shape[0]
    first_channel = (seq_pos * own).astype(jnp.int32).reshape(1)
    table = jnp.asarray(dft_tables(q))

    parts = 4
    outgoing = pl.pallas_call(
        functools.partial(turn_kernel, parts),
        out_shape=jax.ShapeDtypeStruct((channels, q), F32),
        in_specs=[pl.BlockSpec(memory_space=pltpu.HBM)],
        out_specs=pl.BlockSpec(memory_space=pl.ANY),
        scratch_shapes=[
            pltpu.VMEM((q, channels), BF16),
            pltpu.VMEM((channels, q), F32),
            pltpu.SemaphoreType.DMA((parts,)),
            pltpu.SemaphoreType.DMA((parts,)),
        ],
        compiler_params=pltpu.CompilerParams(vmem_limit_bytes=63 * 1024 * 1024),
        cost_estimate=pl.CostEstimate(flops=0, bytes_accessed=6 * q * channels, transcendentals=0),
    )(pltpu.with_memory_space_constraint(values[0], pltpu.HBM))
    incoming = lax.all_to_all(
        outgoing.reshape(seq_count, own, q), "seq", split_axis=0, concat_axis=0, tiled=True
    ).reshape(channels, q)

    depth = -(-(w_in.shape[0] + 1) // 8) * 8
    spectrum, live, turned_gate = call(
        functools.partial(filter_kernel, row_len, q, own),
        [
            jax.ShapeDtypeStruct((channels, 3 * q), F32),
            jax.ShapeDtypeStruct((seq_count, q), F32),
            jax.ShapeDtypeStruct((channels, q), F32),
        ],
        3,
        8,
        scratch=[
            pltpu.VMEM((128, 128), F32),
            pltpu.VMEM((channels, 128), F32),
            pltpu.VMEM((depth, row_len), F32),
            pltpu.VMEM((own, row_len), F32),
            pltpu.VMEM((channels, 2 * q), F32),
        ],
        flops=6 * 2 * row_len * hid * 256 * 8,
        moved=4 * channels * 2 * q,
    )(first_channel, lengths, bands, w_in, b_in.reshape(1, hid), w_mid, w_out, decay.reshape(1, channels),
      skip.reshape(1, channels), gate[0], table)

    convolved = call(
        functools.partial(conv_kernel, q, own),
        jax.ShapeDtypeStruct((channels, q), F32),
        0,
        4,
        scratch=[pltpu.VMEM((channels, 3 * q), F32), pltpu.VMEM((channels, 2 * q), F32)],
        flops=5 * 4 * channels * q * q,
        moved=16 * channels * q,
    )(incoming, live, spectrum, table)
    returned = lax.all_to_all(
        convolved.reshape(seq_count, own, q), "seq", split_axis=0, concat_axis=0, tiled=True
    ).reshape(channels, q)
    halves = 2
    return pl.pallas_call(
        functools.partial(finish_kernel, halves),
        out_shape=jax.ShapeDtypeStruct((q, channels), BF16),
        in_specs=[pl.BlockSpec(memory_space=pltpu.VMEM)] * 2,
        out_specs=pl.BlockSpec(memory_space=pl.ANY),
        scratch_shapes=[pltpu.VMEM((q, channels), BF16), pltpu.SemaphoreType.DMA((halves,))],
        compiler_params=pltpu.CompilerParams(vmem_limit_bytes=8 * 1024 * 1024),
        cost_estimate=pl.CostEstimate(flops=0, bytes_accessed=8 * q * channels, transcendentals=0),
    )(returned, turned_gate)[None]


def solution(mesh):
    split_spec = P("grp", "seq", None)
    return jax.shard_map(
        on_device,
        mesh=mesh,
        in_specs=(split_spec, split_spec, P("grp")) + (P(),) * 7,
        out_specs=split_spec,
        check_vma=False,
    )
```

```python
import functools
import math

import jax
import jax.numpy as jnp
import ml_dtypes
import numpy as np
from jax import lax
from jax.experimental import pallas as pl
from jax.experimental.pallas import tpu as pltpu
from jax.sharding import PartitionSpec as P

F32 = jnp.float32
BF16 = jnp.bfloat16
VMEM_LIMIT = 20 * 1024 * 1024


def split_np(table):
    high = table.astype(np.float32).astype(ml_dtypes.bfloat16)
    low = (table - high.astype(np.float64)).astype(np.float32).astype(ml_dtypes.bfloat16)
    return high, low


def dft_tables(q):
    f = np.arange(q)[None, :]
    n = np.arange(q)[:, None]
    turn = 2.0 * math.pi / (4 * q)
    ahead = ((2 * f + 1) * n % (4 * q)) * turn
    forward = np.concatenate([np.cos(ahead), -np.sin(ahead)], axis=1)
    back = ((2 * f.T + 1) * (n.T + q) % (4 * q)) * turn
    inverse = np.concatenate([np.cos(back), -np.sin(back)], axis=0) / q
    return np.concatenate(
        [*split_np(forward), np.concatenate(split_np(inverse), axis=1)], axis=0
    )


def split(x):
    high = x.astype(BF16)
    return high, (x - high.astype(F32)).astype(BF16)


def dot(a, b, precision=None):
    return lax.dot_general(
        a, b, (((1,), (0,)), ((), ())), precision=precision, preferred_element_type=F32
    )


def dot3(a, b_high, b_low):
    a_high, a_low = split(a)
    return dot(a_high, b_high) + dot(a_low, b_high) + dot(a_high, b_low)


PI_A = 3.140625
PI_B = 9.67502593994140625e-4
PI_C = math.pi - PI_A - PI_B


def odd_fit(func, reach, terms):
    nodes = np.cos(np.pi * (np.arange(400) + 0.5) / 400) * reach
    nodes = nodes[nodes > 0]
    basis = np.stack([nodes ** (2 * i + 1) for i in range(terms)], axis=1)
    weight = 1.0 / nodes[:, None] ** 0.5
    return np.linalg.lstsq(basis * weight, func(nodes) * weight[:, 0], rcond=None)[0]


def even_fit(func, reach, terms):
    nodes = np.cos(np.pi * (np.arange(400) + 0.5) / 400) * reach
    basis = np.stack([nodes ** (2 * i) for i in range(terms)], axis=1)
    return np.linalg.lstsq(basis, func(nodes), rcond=None)[0]


SIN_HALF = [float(c) for c in odd_fit(np.sin, math.pi / 2, 6)]
SIN_QUARTER = [float(c) for c in odd_fit(np.sin, math.pi / 4, 4)]
COS_QUARTER = [float(c) for c in even_fit(np.cos, math.pi / 4, 5)]


def horner(square, coefficients):
    total = jnp.full_like(square, coefficients[-1])
    for c in coefficients[-2::-1]:
        total = total * square + c
    return total


def sine(x):
    turns = lax.round(x * (1.0 / math.pi), lax.RoundingMethod.TO_NEAREST_EVEN)
    r = ((x - turns * PI_A) - turns * PI_B) - turns * PI_C
    value = r * horner(r * r, SIN_HALF)
    odd = (turns.astype(jnp.int32) & 1) == 1
    return jnp.where(odd, -value, value)


def sine_cosine(step, row_len):
    quarter = row_len // 4
    corner = (step + quarter // 2) // quarter
    r = (step - corner * quarter).astype(F32) * (2.0 * math.pi / row_len)
    square = r * r
    s = r * horner(square, SIN_QUARTER)
    c = horner(square, COS_QUARTER)
    swap = (corner & 1) == 1
    sin_v = jnp.where(swap, c, s)
    cos_v = jnp.where(swap, s, c)
    sin_v = jnp.where((corner & 2) == 2, -sin_v, sin_v)
    cos_v = jnp.where(((corner + 1) & 2) == 2, -cos_v, cos_v)
    return sin_v, cos_v


def turn_kernel(parts, x_ref, o_ref, in_ref, out_ref, in_sem, out_sem):
    each = x_ref.shape[1] // parts
    at = [slice(p * each, (p + 1) * each) for p in range(parts)]
    loads = [
        pltpu.make_async_copy(x_ref.at[:, at[p]], in_ref.at[:, at[p]], in_sem.at[p])
        for p in range(parts)
    ]
    stores = [
        pltpu.make_async_copy(out_ref.at[at[p], :], o_ref.at[at[p], :], out_sem.at[p])
        for p in range(parts)
    ]
    for load in loads:
        load.start()
    for p in range(parts):
        loads[p].wait()
        out_ref[at[p], :] = in_ref[:, at[p]].T.astype(F32)
        stores[p].start()
    for store in stores:
        store.wait()


def filter_kernel(
    row_len, q, own, start_ref, len_ref, bands_ref, w_in_ref, b_in_ref, w_mid_ref, w_out_ref, decay_ref,
    skip_ref, gate_ref, table_ref, g_ref, live_ref, turned_gate_ref, wide_ref, turned_ref, embed_ref, shaped_ref, spec_ref,
):
    hid = w_mid_ref.shape[0]
    bands = bands_ref.shape[0]
    emb = w_in_ref.shape[0]
    channels = w_out_ref.shape[1]
    blocks = row_len // q
    high = lax.Precision.HIGHEST
    spot = lax.broadcasted_iota(jnp.int32, (blocks, q), 0) * q
    spot = spot + lax.broadcasted_iota(jnp.int32, (blocks, q), 1)
    live_ref[...] = jnp.where(spot < len_ref[0], 1.0, 0.0)
    room = len_ref[0] - lax.div(start_ref[0] * q, jnp.int32(own))
    here_live = lax.broadcasted_iota(jnp.int32, (1, q), 1) < room
    turned_gate_ref[...] = jnp.where(here_live, gate_ref[...].T.astype(F32), 0.0)
    depth = embed_ref.shape[0]

    wide_ref[...] = jnp.zeros_like(wide_ref)
    wide_ref[0 : 2 * bands, 0:hid] = w_in_ref[1:emb, :]
    wide_ref[2 * bands : 2 * bands + 1, 0:hid] = w_in_ref[0:1, :]
    wide_ref[2 * bands + 1 : 2 * bands + 2, 0:hid] = b_in_ref[...]
    w_first = wide_ref[...].T[0:hid, 0:depth]
    wide_ref[...] = jnp.zeros_like(wide_ref)
    wide_ref[0:hid, 0:hid] = w_mid_ref[...]
    w_second = wide_ref[...].T[0:hid, 0:hid]
    turned_ref[:, 0:hid] = w_out_ref[...].T
    turned_ref[:, hid : hid + 8] = jnp.broadcast_to(decay_ref[...], (8, channels)).T
    turned_ref[:, hid + 8 : hid + 16] = jnp.broadcast_to(skip_ref[...], (8, channels)).T
    mine = pl.ds(pl.multiple_of(start_ref[0], own), own)
    w_last = turned_ref[mine, 0:hid]
    rate = turned_ref[mine, hid : hid + 1]
    direct = turned_ref[mine, hid + 8 : hid + 9]

    row = lax.broadcasted_iota(jnp.int32, (bands, 128), 0)
    column = jnp.zeros((bands, 128), jnp.int32)
    for k in range(bands):
        column = jnp.where(row == k, bands_ref[k], column)
    column = column[:, 0:1]

    chunk = min(1024, row_len)
    energy = jnp.zeros((own, 1), F32)
    for begin in range(0, row_len, chunk):
        at = slice(begin, begin + chunk)
        position = lax.broadcasted_iota(jnp.int32, (1, chunk), 1) + begin
        time = position.astype(F32) * (1.0 / row_len)
        step = lax.rem(
            (lax.broadcasted_iota(jnp.int32, (bands, chunk), 1) + begin) * column,
            jnp.int32(row_len),
        ) if row_len & (row_len - 1) else (
            (lax.broadcasted_iota(jnp.int32, (bands, chunk), 1) + begin) * column & (row_len - 1)
        )
        sin_v, cos_v = sine_cosine(step, row_len)
        embed_ref[0:bands, at] = sin_v
        embed_ref[bands : 2 * bands, at] = cos_v
        tail = lax.broadcasted_iota(jnp.int32, (depth - 2 * bands, chunk), 0)
        embed_ref[2 * bands : depth, at] = jnp.where(
            tail == 0, time, jnp.where(tail == 1, 1.0, 0.0)
        )
        first = sine(dot(w_first, embed_ref[:, at], high))
        second = sine(dot(w_second, first, high))
        shaped = dot(w_last, second, high) * jnp.exp(-rate * time)
        shaped_ref[:, at] = shaped
        energy = energy + jnp.sum(shaped * shaped, axis=1, keepdims=True)
    scale = lax.rsqrt(energy + 1e-06)
    first_lag = lax.broadcasted_iota(jnp.int32, (own, q), 1) == 0
    rows = [shaped_ref[:, d * q : (d + 1) * q] * scale for d in range(blocks)]
    rows[0] = rows[0] + jnp.where(first_lag, direct, 0.0)
    rows = jnp.concatenate(rows, axis=0)
    spec_ref[...] = dot3(rows, table_ref[0:q, :], table_ref[q : 2 * q, :])
    sign = (1 - 2 * (lax.broadcasted_iota(jnp.int32, (own, q), 1) & 1)).astype(F32)
    for d in range(blocks):
        here = slice(d * own, (d + 1) * own)
        re = sign * spec_ref[here, q : 2 * q]
        im = -sign * spec_ref[here, 0:q]
        if d:
            before = slice((d - 1) * own, d * own)
            re = re + spec_ref[before, 0:q]
            im = im + spec_ref[before, q : 2 * q]
        g_ref[here, 0:q] = re
        g_ref[here, q : 2 * q] = im - re
        g_ref[here, 2 * q : 3 * q] = re + im


def conv_kernel(q, own, x_ref, live_ref, g_ref, table_ref, o_ref, spec_ref, prod_ref):
    blocks = x_ref.shape[0] // own
    groups, lanes, pair = own // 8, 128, 2

    def forward(h):
        rows = [
            x_ref[b * own + h * 8 : b * own + h * 8 + 8, :] * live_ref[b : b + 1, :]
            for b in range(blocks)
        ]
        x = jnp.concatenate(rows, axis=0).astype(BF16)
        high, low = slice(0, q), slice(q, 2 * q)
        re = dot(x, table_ref[high, 0:q]) + dot(x, table_ref[low, 0:q])
        im = dot(x, table_ref[high, q : 2 * q]) + dot(x, table_ref[low, q : 2 * q])
        at = slice(h * blocks * 8, (h + 1) * blocks * 8)
        spec_ref[at, 0:q] = re
        spec_ref[at, q : 2 * q] = im
        spec_ref[at, 2 * q : 3 * q] = re + im

    def multiply(h):
        here = [slice((h * blocks + b) * 8, (h * blocks + b + 1) * 8) for b in range(blocks)]
        there = [slice(b * own + h * 8, b * own + h * 8 + 8) for b in range(blocks)]
        for c in range(0, q, lanes):
            planes = [slice(p * q + c, p * q + c + lanes) for p in range(3)]
            for begin in range(0, blocks, pair):
                total = {}
                for a in range(begin + pair):
                    x_re, x_im, x_sum = (spec_ref[here[a], p] for p in planes)
                    for b in range(max(begin, a), begin + pair):
                        g_re, g_diff, g_sum = (g_ref[there[b - a], p] for p in planes)
                        terms = (g_re * x_sum, g_diff * x_re, g_sum * x_im)
                        total[b] = [t + u for t, u in zip(total[b], terms)] if b in total else terms
                for b in range(begin, begin + pair):
                    both, up, down = total[b]
                    prod_ref[here[b], planes[0]] = both - down
                    prod_ref[here[b], planes[1]] = both + up

    def inverse(h):
        y = dot3(prod_ref[h * blocks * 8 : (h + 1) * blocks * 8, :], table_ref[2 * q : 4 * q, 0:q], table_ref[2 * q : 4 * q, q : 2 * q])
        for b in range(blocks):
            o_ref[b * own + h * 8 : b * own + h * 8 + 8, :] = y[b * 8 : (b + 1) * 8, :]

    forward(0)
    for h in range(groups):
        if h:
            inverse(h - 1)
        if h + 1 < groups:
            forward(h + 1)
        multiply(h)
    inverse(groups - 1)


def finish_kernel(parts, conv_ref, gate_ref, o_ref, out_ref, sem):
    each = gate_ref.shape[0] // parts
    stores = []
    for p in range(parts):
        at = slice(p * each, (p + 1) * each)
        out_ref[:, at] = (conv_ref[at, :] * gate_ref[at, :]).T.astype(BF16)
        stores.append(pltpu.make_async_copy(out_ref.at[:, at], o_ref.at[:, at], sem.at[p]))
        stores[p].start()
    for store in stores:
        store.wait()


def call(body, out, smem, vmem, scratch=(), flops=0, moved=0, **kwargs):
    return pl.pallas_call(
        body,
        out_shape=out,
        in_specs=[pl.BlockSpec(memory_space=pltpu.SMEM)] * smem
        + [pl.BlockSpec(memory_space=pltpu.VMEM)] * vmem,
        out_specs=jax.tree.map(lambda _: pl.BlockSpec(memory_space=pltpu.VMEM), out),
        scratch_shapes=list(scratch),
        compiler_params=pltpu.CompilerParams(vmem_limit_bytes=VMEM_LIMIT),
        cost_estimate=pl.CostEstimate(flops=flops, bytes_accessed=moved, transcendentals=0),
        **kwargs,
    )


def on_device(values, gate, lengths, bands, w_in, b_in, w_mid, w_out, decay, skip):
    seq_count = lax.axis_size("seq")
    seq_pos = lax.axis_index("seq")
    q, channels = values.shape[1:]
    own = channels // seq_count
    row_len = q * seq_count
    hid = w_mid.shape[0]
    first_channel = (seq_pos * own).astype(jnp.int32).reshape(1)
    table = jnp.asarray(dft_tables(q))

    parts = 4
    outgoing = pl.pallas_call(
        functools.partial(turn_kernel, parts),
        out_shape=jax.ShapeDtypeStruct((channels, q), F32),
        in_specs=[pl.BlockSpec(memory_space=pltpu.HBM)],
        out_specs=pl.BlockSpec(memory_space=pl.ANY),
        scratch_shapes=[
            pltpu.VMEM((q, channels), BF16),
            pltpu.VMEM((channels, q), F32),
            pltpu.SemaphoreType.DMA((parts,)),
            pltpu.SemaphoreType.DMA((parts,)),
        ],
        compiler_params=pltpu.CompilerParams(vmem_limit_bytes=63 * 1024 * 1024),
        cost_estimate=pl.CostEstimate(flops=0, bytes_accessed=6 * q * channels, transcendentals=0),
    )(pltpu.with_memory_space_constraint(values[0], pltpu.HBM))
    incoming = lax.all_to_all(
        outgoing.reshape(seq_count, own, q), "seq", split_axis=0, concat_axis=0, tiled=True
    ).reshape(channels, q)

    depth = -(-(w_in.shape[0] + 1) // 8) * 8
    spectrum, live, turned_gate = call(
        functools.partial(filter_kernel, row_len, q, own),
        [
            jax.ShapeDtypeStruct((channels, 3 * q), F32),
            jax.ShapeDtypeStruct((seq_count, q), F32),
            jax.ShapeDtypeStruct((channels, q), F32),
        ],
        3,
        8,
        scratch=[
            pltpu.VMEM((128, 128), F32),
            pltpu.VMEM((channels, 128), F32),
            pltpu.VMEM((depth, row_len), F32),
            pltpu.VMEM((own, row_len), F32),
            pltpu.VMEM((channels, 2 * q), F32),
        ],
        flops=6 * 2 * row_len * hid * 256 * 8,
        moved=4 * channels * 2 * q,
    )(first_channel, lengths, bands, w_in, b_in.reshape(1, hid), w_mid, w_out, decay.reshape(1, channels),
      skip.reshape(1, channels), gate[0], table)

    convolved = call(
        functools.partial(conv_kernel, q, own),
        jax.ShapeDtypeStruct((channels, q), F32),
        0,
        4,
        scratch=[pltpu.VMEM((channels, 3 * q), F32), pltpu.VMEM((channels, 2 * q), F32)],
        flops=5 * 4 * channels * q * q,
        moved=16 * channels * q,
    )(incoming, live, spectrum, table)
    returned = lax.all_to_all(
        convolved.reshape(seq_count, own, q), "seq", split_axis=0, concat_axis=0, tiled=True
    ).reshape(channels, q)
    halves = 2
    return pl.pallas_call(
        functools.partial(finish_kernel, halves),
        out_shape=jax.ShapeDtypeStruct((q, channels), BF16),
        in_specs=[pl.BlockSpec(memory_space=pltpu.VMEM)] * 2,
        out_specs=pl.BlockSpec(memory_space=pl.ANY),
        scratch_shapes=[pltpu.VMEM((q, channels), BF16), pltpu.SemaphoreType.DMA((halves,))],
        compiler_params=pltpu.CompilerParams(vmem_limit_bytes=8 * 1024 * 1024),
        cost_estimate=pl.CostEstimate(flops=0, bytes_accessed=8 * q * channels, transcendentals=0),
    )(returned, turned_gate)[None]


def solution(mesh):
    split_spec = P("grp", "seq", None)
    return jax.shard_map(
        on_device,
        mesh=mesh,
        in_specs=(split_spec, split_spec, P("grp")) + (P(),) * 7,
        out_specs=split_spec,
        check_vma=False,
    )
```
